256 devices in a mesh: ep: 32 (over x, y, core), gd: 8 (over z).
Axes of the slice: x: 4, y: 4, z: 8, core: 2. Of those that a mesh axis runs over, the one named last changes fastest.
Arguments:
- tokens: bfloat16 [2048, 4096], P(('ep', 'gd')), may hold values from -6 to 6
- expert_ids: int32 [2048, 8], P(('ep', 'gd')), may hold values from 0 to 31, all different within a row; in each aligned block of 8 rows (0 to 7, 8 to 15, ...) at most 3 rows name the same one
- combine: float32 [2048, 8], P(('ep', 'gd')), may hold values from 0.02 to 0.3
- w_gate: bfloat16 [32, 4096, 1536], P('ep', None, 'gd'), may hold values from -0.09375 to 0.09375
- w_up: bfloat16 [32, 4096, 1536], P('ep', None, 'gd'), may hold values from -0.09375 to 0.09375
- w_down: bfloat16 [32, 1536, 4096], P('ep', 'gd'), may hold values from -0.15625 to 0.15625
- w_query: bfloat16 [4096, 4096], P(None, 'gd'), may hold values from -0.09375 to 0.09375
- w_key: bfloat16 [4096, 1024], P(None, 'gd'), may hold values from -0.09375 to 0.09375
- w_value: bfloat16 [4096, 1024], P(None, 'gd'), may hold values from -0.09375 to 0.09375
- cache_keys: bfloat16 [2048, 8, 64, 128], P('ep', 'gd'), may hold values from -68 to 68
- cache_values: bfloat16 [2048, 8, 64, 128], P('ep', 'gd'), may hold values from -6 to 6
- lengths: int32 [2048], P('ep'), may hold values from 1 to 64, as said below
Outputs:
- stream: bfloat16 [2048, 4096], P(('ep', 'gd'))
- guard: bfloat16 [2048, 4096], P('ep', 'gd')
The draws below stay inside these ranges and needn't reach their ends.
Inputs may be any that keep to these rules, and one draw needn't show every extreme that they name: `expert_ids`: each row names 8 different experts; in the rows of one device no expert is named by more than 3 rows. `lengths`: some row has the full window of 64 positions.
All inputs are finite; a program needn't handle non-finite values.
Results may differ from the reference program's by a relative error of at most 0.03.
Values may be sent and summed in bfloat16 or wider, within the bound.
No kernel may reach another device: no remote copies, remote signals or barrier semaphores. Data moves between devices by JAX's collectives and lax.ppermute only.
A program may use at most 128 MiB of HBM per device.

```python
import math
import jax
import jax.numpy as jnp
import numpy as np
from jax import lax

D = 4096
FF = 1536
HD = 128
GROUP = 4
WIN = 64
ROWS_DEV = 8
EXPERTS = 32
TOP = 8
CAP = 3
TOKENS = 2048
KVH = 8
HQ = 32
N_GD = 8


def draw_lengths(key, part):
    window_len = jax.random.randint(key, (TOKENS,), 1, WIN + 1).astype(jnp.int32)
    longest = jax.random.randint(jax.random.fold_in(key, 11), (), 0, TOKENS)
    shortest = (longest + 1 + jax.random.randint(jax.random.fold_in(key, 12), (), 0, TOKENS - 1)) % TOKENS
    window_len = window_len.at[shortest].set(1)
    window_len = window_len.at[longest].set(WIN)
    return window_len.astype(jnp.int32)


def draw_cache_keys(key, part):
    shape_all = (TOKENS, KVH, WIN, HD)
    values = jnp.clip(jax.random.normal(key, shape_all, jnp.float32), -6.0, 6.0)
    return values.astype(jnp.bfloat16)


def block_scale(stream_key, dims, split, low, high):
    level = 1.0
    for position, shards_of in split:
        heights = jax.random.uniform(jax.random.fold_in(jax.random.fold_in(stream_key, 6), position), (shards_of,), jnp.float32, low / len(split), high / len(split))
        level = level * jnp.repeat(jnp.exp(heights), dims[position] // shards_of).reshape((-1,) + (1,) * (len(dims) - 1 - position))
    return level


def shared_out(key, own, number, rows, number_of, top, limit, slope):
    order = jax.random.permutation(key, number_of)
    heavy_load, usual = portions_of(number_of, rows * top, limit, slope, True), portions_of(number_of, rows * top, limit, slope, False)
    places = jnp.arange(number_of)

    def named(sizes, rotation):
        used = int((sizes > 0).sum())
        fixed = max(1, used // 4)
        moved = fixed + (places - fixed + rotation * (used - fixed)) % max(1, number_of - fixed)
        return jnp.zeros((number_of,), jnp.int32).at[order[jnp.where(places < fixed, places, moved)]].set(jnp.asarray(sizes, jnp.int32))

    sizes = jnp.where(number % 4 == 0, named(heavy_load, number // 4), named(usual, number - number // 4 - 1))
    mixed = jax.random.permutation(jax.random.fold_in(own, 3), number_of)
    donor, sink = mixed[0:number_of // 2 * 2:2], mixed[1:number_of // 2 * 2:2]
    margin = jnp.minimum(sizes[donor] - 1, limit - sizes[sink]) // 2
    margin = jnp.where((donor == order[0]) | (sink == order[0]) | (sizes[sink] == 0), 0, jnp.maximum(margin, 0))
    moved = jax.random.randint(jax.random.fold_in(own, 4), (number_of // 2,), 0, 1 << 20) % (margin + 1)
    sizes = sizes.at[donor].add(-moved).at[sink].add(moved)
    items = jnp.searchsorted(jnp.cumsum(sizes), jnp.arange(rows * top), side="right").astype(jnp.int32)
    table = items.reshape(top, rows).T
    table = table[jax.random.permutation(jax.random.fold_in(own, 1), rows)]
    rotation = jax.random.randint(jax.random.fold_in(own, 2), (rows, 1), 0, top)
    return jnp.take_along_axis(table, (jnp.arange(top)[None, :] + rotation) % top, axis=1)


def portions_of(number_of, total, most, slope, full):
    portions = [(1 << 20) // math.isqrt(rank ** slope) + 1 for rank in range(1, number_of + 1)]
    largest = most if full else min(most, max(-(-total // number_of), total * portions[0] // sum(portions)))
    least = 1 if total - largest >= number_of - 1 else 0
    given, surplus = [largest] + [least] * (number_of - 1), total - largest - least * (number_of - 1)
    while surplus > 0:
        movable = [i for i in range(1, number_of) if given[i] < largest] or [i for i in range(1, number_of) if given[i] < most]
        whole, left = sum([portions[i] for i in movable]), surplus
        for i in movable:
            extra = min(most - given[i], max(1, left * portions[i] // whole), surplus)
            given[i] = given[i] + extra
            surplus = surplus - extra
    return np.array(given)


def gaussian(own_key, extent, scale, reach, pieces=(), kind=jnp.bfloat16):
    entries = scale * jax.random.normal(own_key, extent, jnp.float32)
    if pieces:
        entries = entries * block_scale(own_key, extent, pieces, -0.22, 0.18)
    return jnp.clip(entries, -reach, reach).astype(kind)


def setup_inputs(seed: int = 0) -> dict:
    streams_of = jax.random.split(jax.random.key(seed), 13)
    tokens = gaussian(streams_of[0], (TOKENS, D), 1.0, 6.0, ((0, 256),))
    expert_ids_keys = jax.random.split(jax.random.fold_in(streams_of[1], 1), TOKENS // ROWS_DEV)
    expert_ids_turns = jax.random.permutation(jax.random.fold_in(streams_of[1], 3), TOKENS // ROWS_DEV)
    expert_ids = jax.vmap(lambda own, number: shared_out(jax.random.fold_in(streams_of[1], 2), own, number, ROWS_DEV, EXPERTS, TOP, CAP, 2))(expert_ids_keys, expert_ids_turns).reshape((TOKENS, TOP))
    combine = jnp.clip(0.02 + 0.28 * jax.random.uniform(streams_of[2], (TOKENS, TOP), jnp.float32) ** block_scale(streams_of[2], (TOKENS, TOP), ((0, 256),), -0.2, 0.2), 0.02, 0.3)
    w_gate = gaussian(streams_of[3], (EXPERTS, D, FF), D ** -0.5, 0.09375, ((0, 32), (2, 8)))
    w_up = gaussian(streams_of[4], (EXPERTS, D, FF), D ** -0.5, 0.09375, ((0, 32), (2, 8)))
    w_down = gaussian(streams_of[5], (EXPERTS, FF, D), FF ** -0.5, 0.15625, ((0, 32), (1, 8)))
    w_query = gaussian(streams_of[6], (D, HQ * HD), D ** -0.5, 0.09375, ((1, 8),))
    w_key = gaussian(streams_of[7], (D, KVH * HD), D ** -0.5, 0.09375, ((1, 8),))
    w_value = gaussian(streams_of[8], (D, KVH * HD), D ** -0.5, 0.09375, ((1, 8),))
    cache_keys = draw_cache_keys(jax.random.fold_in(streams_of[12], 71), 0)
    cache_values = gaussian(streams_of[10], (TOKENS, KVH, WIN, HD), 1.0, 6.0, ((0, 32), (1, 8)))
    lengths = draw_lengths(jax.random.fold_in(streams_of[12], 71), 0)
    return dict(tokens=tokens, expert_ids=expert_ids, combine=combine, w_gate=w_gate, w_up=w_up, w_down=w_down, w_query=w_query, w_key=w_key, w_value=w_value, cache_keys=cache_keys, cache_values=cache_values, lengths=lengths)


EPSILON = 1e-06

def norm_rows(values):
    widened = values.astype(jnp.float32)
    return (widened * lax.rsqrt(lax.optimization_barrier(jnp.mean(widened * widened, axis=-1, keepdims=True)) + EPSILON)).astype(jnp.bfloat16)

def slot_numbers(chosen, experts):
    blocks_n, rows_n, picks_n = chosen.shape
    flat_ids = chosen.reshape(blocks_n, rows_n * picks_n)
    onehot = (flat_ids[:, :, None] == jnp.arange(experts, dtype=jnp.int32)[None, None, :]).astype(jnp.int32)
    before = jnp.cumsum(onehot, axis=1) - onehot
    return lax.optimization_barrier(jnp.sum(before * onehot, axis=-1)).reshape(blocks_n, rows_n, picks_n).astype(jnp.int32)

def attend(inputs):
    queries, keys_blk, values_blk, key_new, value_new, window = inputs
    scale_factor = 1.0 / math.sqrt(queries.shape[-1])
    scores = jnp.einsum('rhgd,rhjd->rhgj', queries.astype(jnp.float32), keys_blk.astype(jnp.float32), precision=lax.Precision.HIGHEST) * scale_factor
    own_score = jnp.einsum('rhgd,rhd->rhg', queries.astype(jnp.float32), key_new.astype(jnp.float32), precision=lax.Precision.HIGHEST) * scale_factor
    positions = jnp.arange(keys_blk.shape[2], dtype=jnp.int32)
    allowed = positions[None, None, None, :] >= (keys_blk.shape[2] - window)[:, None, None, None]
    masked = jnp.where(allowed, scores, -jnp.inf)
    highest = jnp.maximum(lax.optimization_barrier(jnp.max(masked, axis=-1)), own_score)
    weights = jnp.exp(masked - highest[..., None])
    own_weight = jnp.exp(own_score - highest)
    denominator = lax.optimization_barrier(jnp.sum(weights, axis=-1)) + own_weight
    probabilities = weights / denominator[..., None]
    own_prob = own_weight / denominator
    attended = jnp.einsum('rhgj,rhjd->rhgd', probabilities, values_blk.astype(jnp.float32), precision=lax.Precision.HIGHEST)
    attended = attended + own_prob[..., None] * value_new.astype(jnp.float32)[:, :, None, :]
    return attended.astype(jnp.bfloat16).reshape(queries.shape[0], -1)

def reference(tokens, expert_ids, combine, w_gate, w_up, w_down, w_query, w_key, w_value, cache_keys, cache_values, lengths):
    normed = norm_rows(tokens)
    blocks_n = TOKENS // ROWS_DEV
    chosen = expert_ids.reshape(blocks_n, ROWS_DEV, TOP)
    slot_ids = slot_numbers(chosen, EXPERTS)
    block_ids = jnp.arange(blocks_n, dtype=jnp.int32)[:, None, None]
    places = (chosen * (blocks_n * CAP) + block_ids * CAP + slot_ids).reshape(-1)
    row_ids = jnp.broadcast_to(jnp.arange(TOKENS, dtype=jnp.int32).reshape(blocks_n, ROWS_DEV, 1), chosen.shape).reshape(-1)
    slot_table = jnp.full((EXPERTS * blocks_n * CAP,), TOKENS, jnp.int32).at[places].set(row_ids)
    slot_table = slot_table.reshape(EXPERTS, blocks_n * CAP)
    weight_table = jnp.zeros((EXPERTS * blocks_n * CAP,), jnp.float32).at[places].set(combine.reshape(-1))
    weight_table = weight_table.reshape(EXPERTS, blocks_n * CAP)
    padded = jnp.concatenate([normed, jnp.zeros((1, D), jnp.bfloat16)], axis=0)
    hidden_group = FF // N_GD

    def expert_step(mixture, inputs):
        gate_w, up_w, down_w, indices, slot_weights = inputs
        picked = padded[indices]
        gate_val = jnp.dot(picked, gate_w, preferred_element_type=jnp.float32)
        up_val = jnp.dot(picked, up_w, preferred_element_type=jnp.float32)
        active = (jax.nn.silu(gate_val) * up_val).astype(jnp.bfloat16)
        result = jnp.zeros((indices.shape[0], D), jnp.float32)
        for member in range(N_GD):
            lower_edge = member * hidden_group
            partial_out = jnp.dot(active[:, lower_edge:lower_edge + hidden_group], down_w[lower_edge:lower_edge + hidden_group], preferred_element_type=jnp.float32).astype(jnp.bfloat16)
            result = result + partial_out.astype(jnp.float32)
        mixture = mixture.at[indices].add(slot_weights[:, None] * result)
        return (mixture, None)
    mixture, unused = lax.scan(expert_step, jnp.zeros((TOKENS + 1, D), jnp.float32), (w_gate, w_up, w_down, slot_table, weight_table))
    stream = (tokens.astype(jnp.float32) + mixture[:TOKENS]).astype(jnp.bfloat16)
    guard_norm = norm_rows(stream)
    queries = jnp.dot(guard_norm, w_query, preferred_element_type=jnp.float32)
    key_new = jnp.dot(guard_norm, w_key, preferred_element_type=jnp.float32).astype(jnp.bfloat16)
    value_new = jnp.dot(guard_norm, w_value, preferred_element_type=jnp.float32).astype(jnp.bfloat16)
    group_rows = ROWS_DEV * N_GD
    count_blocks = TOKENS // group_rows
    guard = lax.map(attend, (queries.reshape(count_blocks, group_rows, KVH, GROUP, HD), cache_keys.reshape(count_blocks, group_rows, KVH, WIN, HD), cache_values.reshape(count_blocks, group_rows, KVH, WIN, HD), key_new.reshape(count_blocks, group_rows, KVH, HD), value_new.reshape(count_blocks, group_rows, KVH, HD), lengths.reshape(count_blocks, group_rows)))
    return (stream, guard.reshape(TOKENS, HQ * HD))
```

```python
import functools
import math

import jax
import jax.numpy as jnp
from jax import lax
from jax.experimental import pallas as pl
from jax.experimental.pallas import tpu as pltpu
from jax.sharding import Mesh
from jax.sharding import PartitionSpec as P

EPSILON = 1e-06
BF = jnp.bfloat16
F32 = jnp.float32
LANES = 128
CAP = 3


def shift(values, axis, step):
    size = lax.axis_size(axis)
    return lax.ppermute(values, axis, [(i, (i - step) % size) for i in range(size)])


def copies(values, axis):
    size = lax.axis_size(axis)
    return lax.all_to_all(
        jnp.broadcast_to(values[None], (size, *values.shape)), axis, 0, 0, tiled=True
    )


def ring4(block, axis):
    half = block.shape[0] // 2
    after, before = shift(block, axis, 1), shift(block, axis, -1)
    first, second = shift(before[:half], axis, -1), shift(after[half:], axis, 1)
    return block, after, first, second, before


def expert_kernel(sizes, steps, place_ref, mask_ref, *refs):
    n = len(sizes)
    rows, meta = refs[:n], refs[n : 2 * n]
    own_ref, other_ref = refs[2 * n : 2 * n + 2]
    outs = refs[2 * n + 2 : 3 * n + 2]
    totals = refs[3 * n + 2 :]
    k = pl.program_id(0)
    for i in range(n):
        x = rows[i][...]
        for j, w_ref in enumerate((own_ref, other_ref)):
            part = jnp.dot(x, w_ref[...], preferred_element_type=F32)

            @pl.when(k == 0)
            def _():
                totals[2 * i + j][...] = part

            @pl.when(k > 0)
            def _():
                totals[2 * i + j][...] += part

    @pl.when(k == steps - 1)
    def _():
        for i, (m, inner) in enumerate(sizes):
            slots = m // 8 * CAP
            per = m // inner
            per_slots = per // 8 * CAP
            r = lax.broadcasted_iota(jnp.int32, (m, slots), 0)
            s = lax.broadcasted_iota(jnp.int32, (m, slots), 1)
            group = s // per_slots
            if inner == 4:
                group = (group + 4 - place_ref[i]) % 4
            elif inner == 2:
                group = (group + place_ref[i]) % 2
            block = group * (per // 8) + s % per_slots // CAP
            same = r // 8 == block
            rank = (s % CAP).astype(F32)
            both = []
            for j in range(2):
                total = totals[2 * i + j][...]
                hidden = total.shape[1] // 2
                gate, up = total[:, :hidden], total[:, hidden:]
                active = (gate / (1.0 + jnp.exp(-gate)) * up).astype(BF)
                held = jnp.sum(
                    meta[i][...].astype(F32) * mask_ref[j : j + 1, :], axis=1, keepdims=True
                )
                pick = jnp.where(same & (held == rank), 1.0, 0.0).astype(BF)
                both.append(
                    lax.dot_general(
                        pick, active, (((0,), (0,)), ((), ())), preferred_element_type=F32
                    )
                )
            outs[i][...] = jnp.concatenate(both, axis=1).astype(BF)


def expert_slots(pieces, inners, places, masks, w_own, w_other):
    n = len(pieces)
    depth, cols = w_own.shape
    chunk = 512
    steps = depth // chunk
    sizes = tuple((p.shape[0], inner) for p, inner in zip(pieces, inners))
    in_specs = [
        pl.BlockSpec(memory_space=pltpu.SMEM),
        pl.BlockSpec((8, LANES), lambda k: (0, 0)),
    ]
    in_specs += [pl.BlockSpec((m, chunk), lambda k: (0, k)) for m, _ in sizes]
    in_specs += [pl.BlockSpec((m, LANES), lambda k: (0, depth // LANES)) for m, _ in sizes]
    in_specs += [pl.BlockSpec((chunk, cols), lambda k: (k, 0))] * 2
    slots = [m // 8 * CAP for m, _ in sizes]
    total_rows = sum(m for m, _ in sizes)
    return pl.pallas_call(
        functools.partial(expert_kernel, sizes, steps),
        grid=(steps,),
        in_specs=in_specs,
        out_specs=[pl.BlockSpec((s, cols), lambda k: (0, 0)) for s in slots],
        out_shape=[jax.ShapeDtypeStruct((s, cols), BF) for s in slots],
        scratch_shapes=[pltpu.VMEM((m, cols), F32) for m, _ in sizes for _ in range(2)],
        compiler_params=pltpu.CompilerParams(vmem_limit_bytes=48 << 20),
        cost_estimate=pl.CostEstimate(
            flops=4 * total_rows * depth * cols,
            bytes_accessed=4 * depth * cols + 2 * total_rows * depth,
            transcendentals=total_rows * cols,
        ),
        name="expert_slots",
    )(places, masks, *pieces, *pieces, w_own, w_other)


def attend(group_stream, w_query, w_key, w_value, cache_keys, cache_values, lengths):
    widened = group_stream.astype(F32)
    guard_norm = (
        widened * lax.rsqrt(jnp.mean(widened * widened, axis=-1, keepdims=True) + EPSILON)
    ).astype(BF)
    queries = jnp.dot(guard_norm, w_query, preferred_element_type=F32)
    key_new = jnp.dot(guard_norm, w_key, preferred_element_type=F32).astype(BF)
    value_new = jnp.dot(guard_norm, w_value, preferred_element_type=F32).astype(BF)
    group_total, heads_kv, window_len, head_size = cache_keys.shape
    heads_per = w_query.shape[1] // (heads_kv * head_size)
    queries = queries.reshape(group_total, heads_kv, heads_per, head_size)
    key_new = key_new.reshape(group_total, heads_kv, head_size)
    value_new = value_new.reshape(group_total, heads_kv, head_size)
    scale_factor = 1.0 / math.sqrt(head_size)
    scores = (
        jnp.einsum(
            "rhgd,rhjd->rhgj", queries, cache_keys.astype(F32), precision=lax.Precision.HIGHEST
        )
        * scale_factor
    )
    own_score = (
        jnp.einsum(
            "rhgd,rhd->rhg", queries, key_new.astype(F32), precision=lax.Precision.HIGHEST
        )
        * scale_factor
    )
    positions = jnp.arange(window_len, dtype=jnp.int32)
    allowed = positions[None, None, None, :] >= (window_len - lengths)[:, None, None, None]
    masked = jnp.where(allowed, scores, -jnp.inf)
    highest = jnp.maximum(jnp.max(masked, axis=-1), own_score)
    weights = jnp.exp(masked - highest[..., None])
    own_weight = jnp.exp(own_score - highest)
    denominator = jnp.sum(weights, axis=-1) + own_weight
    probabilities = weights / denominator[..., None]
    own_prob = own_weight / denominator
    attended = jnp.einsum(
        "rhgj,rhjd->rhgd",
        probabilities,
        cache_values.astype(F32),
        precision=lax.Precision.HIGHEST,
    )
    attended = attended + own_prob[..., None] * value_new.astype(F32)[:, :, None, :]
    return attended.astype(BF).reshape(group_total, heads_kv * heads_per * head_size)


def split3(values):
    high = values.astype(BF)
    rest = values - high.astype(F32)
    middle = rest.astype(BF)
    return high, middle, (rest - middle.astype(F32)).astype(BF)


def routing_columns(expert_ids, combine, experts):
    named = expert_ids[:, :, None] == jnp.arange(experts, dtype=jnp.int32)
    chosen = jnp.any(named, axis=1)
    weight = jnp.sum(jnp.where(named, combine[:, :, None], 0.0), axis=1)
    rows = jnp.arange(expert_ids.shape[0])
    earlier = rows[None, :, None] < rows[:, None, None]
    rank = jnp.sum((earlier & chosen[None]).astype(jnp.int32), axis=1)
    rank = jnp.where(chosen, rank, CAP).astype(BF)
    return jnp.concatenate([rank, *split3(weight)], axis=1)


def per_device(
    tokens,
    expert_ids,
    combine,
    w_gate,
    w_up,
    w_down,
    w_query,
    w_key,
    w_value,
    cache_keys,
    cache_values,
    lengths,
):
    rows_n, width = tokens.shape
    x, y, c, z = (lax.axis_index(a) for a in ("x", "y", "c", "z"))
    chips = lax.axis_size("x") * lax.axis_size("y")
    experts = 2 * chips
    members = lax.axis_size("z")
    group = rows_n * members
    hidden = w_gate.shape[2]
    cols = width // members

    w_own = jnp.concatenate([w_gate[0], w_up[0]], axis=1)
    w_other = shift(w_own, "c", 1)
    down = w_down[0]
    parts = []
    for d in range(members):
        block = lax.dynamic_slice(
            down, (jnp.int32(0), (z - d) % members * cols), (hidden, cols)
        )
        parts.append(block if d == 0 else shift(block, "z", d))
    down_own = jnp.stack(parts)
    down_other = shift(down_own, "c", 1)

    sent = jnp.concatenate([tokens, routing_columns(expert_ids, combine, experts)], axis=1)
    arrived = copies(sent, "z").reshape(group, width + LANES)
    group_tokens, meta = arrived[:, :width], arrived[:, width:]
    widened = group_tokens.astype(F32)
    normed = (
        widened * lax.rsqrt(jnp.mean(widened * widened, axis=-1, keepdims=True) + EPSILON)
    ).astype(BF)
    dense = jnp.concatenate([normed, meta], axis=1)

    lane = jnp.arange(LANES, dtype=jnp.int32)[None, :]
    e_own = (x * 4 + y) * 2 + c
    e_other = (x * 4 + y) * 2 + 1 - c
    masks = jnp.concatenate([lane == e_own, lane == e_other] + [lane < 0] * 6, axis=0).astype(F32)
    half = group // 2
    a_first = jnp.concatenate(ring4(dense[:half], "x"), axis=0)
    b_first = jnp.concatenate(ring4(dense[half:], "y"), axis=0)
    a0, a1, a2, a3, a4 = ring4(a_first, "y")
    b0, b1, b2, b3, b4 = ring4(b_first, "x")
    i32 = lambda *v: jnp.stack([jnp.asarray(s, jnp.int32) for s in v])
    zero = jnp.int32(0)
    sa0, sb0 = expert_slots((a0, b0), (4, 4), i32(x, y), masks, w_own, w_other)
    sa1, sa4, sb1, sb4 = expert_slots(
        (a1, a4, b1, b4), (4, 4, 4, 4), i32(x, x, y, y), masks, w_own, w_other
    )
    sa2, sa3, sb2, sb3 = expert_slots(
        (a2, a3, b2, b3), (1, 1, 1, 1), i32(zero, zero, zero, zero), masks, w_own, w_other
    )
    per_group = half // 8 * CAP

    def opposite(first, second, place):
        both = jnp.concatenate([first, second], axis=0).reshape(4, per_group, -1)
        return jnp.roll(both, place, axis=0).reshape(4 * per_group, -1)

    slots_a = jnp.roll(jnp.stack([sa0, sa1, opposite(sa2, sa3, x), sa4]), y, axis=0)
    slots_b = jnp.roll(jnp.stack([sb0, sb1, opposite(sb2, sb3, y), sb4]), x, axis=0)
    slots_a = slots_a.reshape(4, 4, per_group, 2 * hidden).transpose(1, 0, 2, 3)
    slots_b = slots_b.reshape(4, 4, per_group, 2 * hidden)
    slots = jnp.stack([slots_a, slots_b], axis=2).reshape(chips * 2 * per_group, 2 * hidden)

    pieces = [slots] + [None] * (members - 1)
    after = before = slots
    for d in range(1, members // 2):
        after, before = shift(after, "z", 1), shift(before, "z", -1)
        pieces[d], pieces[members - d] = after, before
    mid = slots.shape[0] // 2
    pieces[members // 2] = jnp.concatenate(
        [shift(after[:mid], "z", 1), shift(before[mid:], "z", -1)], axis=0
    )
    active = jnp.stack(pieces)
    out_own = jnp.einsum(
        "dsf,dfn->sn", active[:, :, :hidden], down_own, preferred_element_type=F32
    )
    out_other = jnp.einsum(
        "dsf,dfn->sn", active[:, :, hidden:], down_other, preferred_element_type=F32
    )
    per_chip = 2 * per_group
    result = jnp.stack(
        [
            out_own.astype(BF).reshape(chips, per_chip, cols),
            out_other.astype(BF).reshape(chips, per_chip, cols),
        ],
        axis=1,
    ).reshape(chips, 2 * per_chip, cols)
    returned = lax.all_to_all(result, ("x", "y"), 0, 0, tiled=True)

    rank = meta[:, :experts].astype(F32)
    weight = sum(meta[:, i * experts : (i + 1) * experts].astype(F32) for i in (1, 2, 3))
    by_core = lambda v: v.reshape(group, chips, 2)
    order = lambda v: jnp.where(c == 0, by_core(v), by_core(v)[:, :, ::-1])
    rank, weight = order(rank), order(weight)
    slot = jnp.arange(per_chip, dtype=jnp.int32)
    mine = (slot // CAP)[None, :] == (jnp.arange(group) // rows_n)[:, None]
    hit = mine[:, None, None, :] & (
        rank[..., None] == (slot % CAP).astype(F32)[None, None, None, :]
    )
    spread = jnp.where(hit, weight[..., None], 0.0).reshape(group, chips * 2 * per_chip)
    mixture = jnp.dot(
        spread,
        returned.reshape(chips * 2 * per_chip, cols).astype(F32),
        precision=lax.Precision.HIGHEST,
        preferred_element_type=F32,
    )
    block_tokens = lax.dynamic_slice(group_tokens, (jnp.int32(0), z * cols), (group, cols))
    stream_block = (block_tokens.astype(F32) + mixture).astype(BF)
    group_stream = copies(stream_block, "z").transpose(1, 0, 2).reshape(group, width)
    stream = lax.dynamic_slice(group_stream, (z * rows_n, jnp.int32(0)), (rows_n, width))
    guard = attend(group_stream, w_query, w_key, w_value, cache_keys, cache_values, lengths)
    return (stream, guard)


def solution(mesh):
    torus = Mesh(mesh.devices.reshape(4, 4, 2, mesh.devices.shape[1]), ("x", "y", "c", "z"))
    ep = ("x", "y", "c")
    every = (*ep, "z")
    return jax.shard_map(
        per_device,
        mesh=torus,
        in_specs=(
            P(every, None),
            P(every, None),
            P(every, None),
            P(ep, None, "z"),
            P(ep, None, "z"),
            P(ep, "z", None),
            P(None, "z"),
            P(None, "z"),
            P(None, "z"),
            P(ep, "z", None, None),
            P(ep, "z", None, None),
            P(ep),
        ),
        out_specs=(P(every, None), P(ep, "z")),
        check_vma=False,
    )
```

```python
import functools
import math

import jax
import jax.numpy as jnp
from jax import lax
from jax.experimental import pallas as pl
from jax.experimental.pallas import tpu as pltpu
from jax.sharding import Mesh
from jax.sharding import PartitionSpec as P

EPSILON = 1e-06
BF = jnp.bfloat16
F32 = jnp.float32
LANES = 128
CAP = 3


def shift(values, axis, step):
    size = lax.axis_size(axis)
    return lax.ppermute(values, axis, [(i, (i - step) % size) for i in range(size)])


def copies(values, axis):
    size = lax.axis_size(axis)
    return lax.all_to_all(
        jnp.broadcast_to(values[None], (size, *values.shape)), axis, 0, 0, tiled=True
    )


def expert_kernel(sizes, early, steps, place_ref, mask_ref, *refs):
    n = len(sizes)
    rows, meta = refs[:n], refs[n : 2 * n]
    w_refs = refs[2 * n : 2 * n + 4]
    out_ref, joined, totals = refs[2 * n + 4 :]
    k = pl.program_id(0)
    hidden = w_refs[0].shape[0]
    at = 0
    for m, row_ref in zip(sizes, rows):
        joined[at : at + m, :] = row_ref[...]
        at += m
    part = lax.dot_general(
        joined[...],
        jnp.concatenate([w_ref[...] for w_ref in w_refs], axis=0),
        (((1,), (1,)), ((), ())),
        preferred_element_type=F32,
    )

    @pl.when(k == 0)
    def _():
        totals[...] = part

    @pl.when(k > 0)
    def _():
        totals[...] += part

    @pl.when(k == steps - 1)
    def _():
        slots = out_ref.shape[0]
        held = lax.dot_general(
            mask_ref[...],
            jnp.concatenate([m_ref[...] for m_ref in meta], axis=0),
            (((1,), (1,)), ((), ())),
            preferred_element_type=F32,
        )
        s = lax.broadcasted_iota(jnp.int32, (slots, 1), 0)
        if early:
            piece = slots // 6
            per = piece // 4
            place = jnp.where(s < slots // 2, place_ref[0], place_ref[1])
            inner = (s % piece // per + 4 - place) % 4
            block = s // piece * (piece // CAP) + inner * (per // CAP) + s % per // CAP
        else:
            block = s // CAP
        same = lax.broadcasted_iota(jnp.int32, (slots, at), 1) // 8 == block
        rank = (s % CAP).astype(F32)
        for j in range(2):
            base = 2 * j * hidden
            gate = totals[:, base : base + hidden]
            up = totals[:, base + hidden : base + 2 * hidden]
            active = (gate / (1.0 + jnp.exp(-gate)) * up).astype(BF)
            pick = jnp.where(same & (held[j : j + 1, :] == rank), 1.0, 0.0).astype(BF)
            packed = jnp.dot(pick, active, preferred_element_type=F32)
            out_ref[:, j * hidden : (j + 1) * hidden] = packed.astype(BF)


def expert_slots(pieces, early, place, masks, weights):
    hidden, depth = weights[0].shape
    chunk = 1024
    steps = depth // chunk
    sizes = tuple(p.shape[0] for p in pieces)
    in_specs = [
        pl.BlockSpec(memory_space=pltpu.SMEM),
        pl.BlockSpec((8, LANES), lambda k: (0, 0)),
    ]
    in_specs += [pl.BlockSpec((m, chunk), lambda k: (0, k)) for m in sizes]
    in_specs += [pl.BlockSpec((m, LANES), lambda k: (0, depth // LANES)) for m in sizes]
    in_specs += [pl.BlockSpec((hidden, chunk), lambda k: (0, k))] * 4
    total = sum(sizes)
    slots = total // 8 * CAP
    return pl.pallas_call(
        functools.partial(expert_kernel, sizes, early, steps),
        grid=(steps,),
        in_specs=in_specs,
        out_specs=pl.BlockSpec((slots, 2 * hidden), lambda k: (0, 0)),
        out_shape=jax.ShapeDtypeStruct((slots, 2 * hidden), BF),
        scratch_shapes=[
            pltpu.VMEM((total, chunk), BF),
            pltpu.VMEM((total, 4 * hidden), F32),
        ],
        compiler_params=pltpu.CompilerParams(vmem_limit_bytes=20 << 20),
        cost_estimate=pl.CostEstimate(
            flops=8 * total * depth * hidden,
            bytes_accessed=8 * depth * hidden + 2 * total * depth,
            transcendentals=2 * total * hidden,
        ),
        name="expert_slots",
    )(place, masks, *pieces, *pieces, *weights)


def lower_kernel(place_ref, early_ref, late_ref, own_ref, other_ref, out_ref, *sums):
    members, first, _ = early_ref.shape
    hidden = own_ref.shape[1]
    for j, w_ref in enumerate((own_ref, other_ref)):
        for d in range(members):
            span = slice(j * hidden, (j + 1) * hidden)
            active = jnp.concatenate([early_ref[d][:, span], late_ref[d][:, span]], axis=0)
            part = jnp.dot(active, w_ref[d], preferred_element_type=F32)
            if d == 0:
                sums[j][...] = part
            else:
                sums[j][...] += part
    x, y = place_ref[0], place_ref[1]
    placed = sums[2]
    per = placed.shape[2] // 2
    for h in range(2):
        for o, step in enumerate((0, 1, 3, 2)):
            for i in range(4):
                at = (3 * h + o) * 4 * per if o < 3 else first + h * 4 * per
                at = at + i * per
                if h == 0:
                    inner = i if o < 3 else (x + i) % 4
                    chip = inner * 4 + (y + step) % 4
                else:
                    inner = i if o < 3 else (y + i) % 4
                    chip = (x + step) % 4 * 4 + inner
                for j in range(2):
                    placed[chip, j, h * per : (h + 1) * per, :] = sums[j][at : at + per, :]
    out_ref[...] = placed[...].astype(BF)


def lower(place, early, late, down_own, down_other, chips):
    members, first, width = early.shape
    slots = first + late.shape[1]
    cols = down_own.shape[2]
    per_chip = slots // chips
    return pl.pallas_call(
        lower_kernel,
        in_specs=[pl.BlockSpec(memory_space=pltpu.SMEM)]
        + [pl.BlockSpec(memory_space=pltpu.VMEM)] * 4,
        out_specs=pl.BlockSpec(memory_space=pltpu.VMEM),
        out_shape=jax.ShapeDtypeStruct((chips, 2, per_chip, cols), BF),
        scratch_shapes=[
            pltpu.VMEM((slots, cols), F32),
            pltpu.VMEM((slots, cols), F32),
            pltpu.VMEM((chips, 2, per_chip, cols), F32),
        ],
        compiler_params=pltpu.CompilerParams(vmem_limit_bytes=16 << 20),
        cost_estimate=pl.CostEstimate(
            flops=2 * members * slots * width * cols,
            bytes_accessed=2 * members * width * (slots + cols),
            transcendentals=0,
        ),
        name="lower",
    )(place, early, late, down_own, down_other)


def attend(group_stream, w_query, w_key, w_value, cache_keys, cache_values, lengths):
    widened = group_stream.astype(F32)
    guard_norm = (
        widened * lax.rsqrt(jnp.mean(widened * widened, axis=-1, keepdims=True) + EPSILON)
    ).astype(BF)
    queries = jnp.dot(guard_norm, w_query, preferred_element_type=F32)
    key_new = jnp.dot(guard_norm, w_key, preferred_element_type=F32).astype(BF)
    value_new = jnp.dot(guard_norm, w_value, preferred_element_type=F32).astype(BF)
    group_total, heads_kv, window_len, head_size = cache_keys.shape
    heads_per = w_query.shape[1] // (heads_kv * head_size)
    queries = queries.reshape(group_total, heads_kv, heads_per, head_size)
    key_new = key_new.reshape(group_total, heads_kv, head_size)
    value_new = value_new.reshape(group_total, heads_kv, head_size)
    scale_factor = 1.0 / math.sqrt(head_size)
    scores = (
        jnp.einsum(
            "rhgd,rhjd->rhgj", queries, cache_keys.astype(F32), precision=lax.Precision.HIGHEST
        )
        * scale_factor
    )
    own_score = (
        jnp.einsum(
            "rhgd,rhd->rhg", queries, key_new.astype(F32), precision=lax.Precision.HIGHEST
        )
        * scale_factor
    )
    positions = jnp.arange(window_len, dtype=jnp.int32)
    allowed = positions[None, None, None, :] >= (window_len - lengths)[:, None, None, None]
    masked = jnp.where(allowed, scores, -jnp.inf)
    highest = jnp.maximum(jnp.max(masked, axis=-1), own_score)
    weights = jnp.exp(masked - highest[..., None])
    own_weight = jnp.exp(own_score - highest)
    denominator = jnp.sum(weights, axis=-1) + own_weight
    probabilities = weights / denominator[..., None]
    own_prob = own_weight / denominator
    attended = jnp.einsum(
        "rhgj,rhjd->rhgd",
        probabilities,
        cache_values.astype(F32),
        precision=lax.Precision.HIGHEST,
    )
    attended = attended + own_prob[..., None] * value_new.astype(F32)[:, :, None, :]
    return attended.astype(BF).reshape(group_total, heads_kv * heads_per * head_size)


def split3(values):
    high = values.astype(BF)
    rest = values - high.astype(F32)
    middle = rest.astype(BF)
    return high, middle, (rest - middle.astype(F32)).astype(BF)


def routing_columns(expert_ids, combine, experts):
    named = expert_ids[:, :, None] == jnp.arange(experts, dtype=jnp.int32)
    chosen = jnp.any(named, axis=1)
    weight = jnp.sum(jnp.where(named, combine[:, :, None], 0.0), axis=1)
    rows = jnp.arange(expert_ids.shape[0])
    earlier = rows[None, :, None] < rows[:, None, None]
    rank = jnp.sum((earlier & chosen[None]).astype(jnp.int32), axis=1)
    rank = jnp.where(chosen, rank, CAP).astype(BF)
    return jnp.concatenate([rank, *split3(weight)], axis=1)


def per_device(
    tokens,
    expert_ids,
    combine,
    w_gate,
    w_up,
    w_down,
    w_query,
    w_key,
    w_value,
    cache_keys,
    cache_values,
    lengths,
):
    rows_n, width = tokens.shape
    x, y, c, z = (lax.axis_index(a) for a in ("x", "y", "c", "z"))
    chips = lax.axis_size("x") * lax.axis_size("y")
    experts = 2 * chips
    members = lax.axis_size("z")
    group = rows_n * members
    hidden = w_gate.shape[2]
    cols = width // members

    own = [w_gate[0].T, w_up[0].T]
    weights = own + [shift(w, "c", 1) for w in own]

    sent = jnp.concatenate([tokens, routing_columns(expert_ids, combine, experts)], axis=1)
    arrived = copies(sent, "z").reshape(group, width + LANES)
    group_tokens, meta = arrived[:, :width], arrived[:, width:]
    widened = group_tokens.astype(F32)
    normed = (
        widened * lax.rsqrt(jnp.mean(widened * widened, axis=-1, keepdims=True) + EPSILON)
    ).astype(BF)
    dense = jnp.concatenate([normed, meta], axis=1)

    lane = jnp.arange(LANES, dtype=jnp.int32)[None, :]
    e_own = (x * 4 + y) * 2 + c
    e_other = (x * 4 + y) * 2 + 1 - c
    masks = jnp.concatenate([lane == e_own, lane == e_other] + [lane < 0] * 6, axis=0).astype(F32)
    masks = masks.astype(BF)
    half = group // 2

    def first_ring(block, axis):
        mid = block.shape[0] // 2
        after, before = shift(block, axis, 1), shift(block, axis, -1)
        near = jnp.concatenate([block, after], axis=0)
        opposite = shift(before[:mid], axis, -1), shift(after[mid:], axis, 1)
        return near, jnp.concatenate([*opposite, before], axis=0)

    def second_ring(near, far, axis):
        near_after, near_before = shift(near, axis, 1), shift(near, axis, -1)
        far_after, far_before = shift(far, axis, 1), shift(far, axis, -1)
        opposite = shift(near_before, axis, -1), shift(far_after, axis, 1)
        return (near, far, near_after, far_after, near_before, far_before), opposite

    a_near, a_far = first_ring(dense[:half], "x")
    b_near, b_far = first_ring(dense[half:], "y")
    a_far, b_far, *weights = lax.optimization_barrier((a_far, b_far, *weights))
    _, _, down = lax.optimization_barrier((a_far[:8], b_far[:8], w_down[0]))
    down_own = lax.all_to_all(down, "z", 1, 0, tiled=True)
    down_own = down_own.reshape(members, hidden, cols)
    down_other = shift(down_own, "c", 1)
    a_early, a_late = second_ring(a_near, a_far, "y")
    b_early, b_late = second_ring(b_near, b_far, "x")
    place = jnp.stack([x, y]).astype(jnp.int32)
    early = expert_slots((*a_early, *b_early), True, place, masks, weights)
    early, *rest = lax.optimization_barrier((early, *a_late, *b_late))
    late = expert_slots(rest, False, place, masks, weights)
    early = lax.all_gather(early, "z", axis=0)
    late = copies(late, "z")
    result = lower(place, early, late, down_own, down_other, chips)
    per_chip = result.shape[2]
    result = result.reshape(chips, 2 * per_chip, cols)
    returned = lax.all_to_all(result, ("x", "y"), 0, 0, tiled=True)

    rank = meta[:, :experts].astype(F32)
    weight = sum(meta[:, i * experts : (i + 1) * experts].astype(F32) for i in (1, 2, 3))
    by_core = lambda v: v.reshape(group, chips, 2)
    order = lambda v: jnp.where(c == 0, by_core(v), by_core(v)[:, :, ::-1])
    rank, weight = order(rank), order(weight)
    slot = jnp.arange(per_chip, dtype=jnp.int32)
    mine = (slot // CAP)[None, :] == (jnp.arange(group) // rows_n)[:, None]
    hit = mine[:, None, None, :] & (
        rank[..., None] == (slot % CAP).astype(F32)[None, None, None, :]
    )
    spread = jnp.where(hit, weight[..., None], 0.0).reshape(group, chips * 2 * per_chip)
    mixture = jnp.dot(
        spread,
        returned.reshape(chips * 2 * per_chip, cols).astype(F32),
        precision=lax.Precision.HIGHEST,
        preferred_element_type=F32,
    )
    block_tokens = lax.dynamic_slice(group_tokens, (jnp.int32(0), z * cols), (group, cols))
    stream_block = (block_tokens.astype(F32) + mixture).astype(BF)
    group_stream = copies(stream_block, "z").transpose(1, 0, 2).reshape(group, width)
    stream = lax.dynamic_slice(group_stream, (z * rows_n, jnp.int32(0)), (rows_n, width))
    guard = attend(group_stream, w_query, w_key, w_value, cache_keys, cache_values, lengths)
    return (stream, guard)


def solution(mesh):
    torus = Mesh(mesh.devices.reshape(4, 4, 2, mesh.devices.shape[1]), ("x", "y", "c", "z"))
    ep = ("x", "y", "c")
    every = (*ep, "z")
    return jax.shard_map(
        per_device,
        mesh=torus,
        in_specs=(
            P(every, None),
            P(every, None),
            P(every, None),
            P(ep, None, "z"),
            P(ep, None, "z"),
            P(ep, "z", None),
            P(None, "z"),
            P(None, "z"),
            P(None, "z"),
            P(ep, "z", None, None),
            P(ep, "z", None, None),
            P(ep),
        ),
        out_specs=(P(every, None), P(ep, "z")),
        check_vma=False,
    )
```

```python
import functools
import math

import jax
import jax.numpy as jnp
from jax import lax
from jax.experimental import pallas as pl
from jax.experimental.pallas import tpu as pltpu
from jax.sharding import Mesh
from jax.sharding import PartitionSpec as P

EPSILON = 1e-06
BF = jnp.bfloat16
F32 = jnp.float32
LANES = 128
CAP = 3


def shift(values, axis, step):
    size = lax.axis_size(axis)
    return lax.ppermute(values, axis, [(i, (i - step) % size) for i in range(size)])


def ring(block, axis):
    size = lax.axis_size(axis)
    pieces = [block] + [None] * (size - 1)
    after = before = block
    for d in range(1, size // 2):
        after, before = shift(after, axis, 1), shift(before, axis, -1)
        pieces[d], pieces[size - d] = after, before
    mid = block.shape[0] // 2
    farthest = shift(after[:mid], axis, 1), shift(before[mid:], axis, -1)
    pieces[size // 2] = jnp.concatenate(farthest, axis=0)
    return pieces


def copies(values, axis):
    size = lax.axis_size(axis)
    return lax.all_to_all(
        jnp.broadcast_to(values[None], (size, *values.shape)), axis, 0, 0, tiled=True
    )


def expert_kernel(sizes, steps, mask_ref, *refs):
    n = len(sizes)
    rows, meta = refs[:n], refs[n : 2 * n]
    w_refs = refs[2 * n : 2 * n + 4]
    out_ref, joined, totals = refs[2 * n + 4 :]
    k = pl.program_id(0)
    hidden = w_refs[0].shape[0]
    at = 0
    for m, row_ref in zip(sizes, rows):
        joined[at : at + m, :] = row_ref[...]
        at += m
    part = lax.dot_general(
        joined[...],
        jnp.concatenate([w_ref[...] for w_ref in w_refs], axis=0),
        (((1,), (1,)), ((), ())),
        preferred_element_type=F32,
    )

    @pl.when(k == 0)
    def _():
        totals[...] = part

    @pl.when(k > 0)
    def _():
        totals[...] += part

    @pl.when(k == steps - 1)
    def _():
        slots = out_ref.shape[0]
        held = lax.dot_general(
            mask_ref[...],
            jnp.concatenate([m_ref[...] for m_ref in meta], axis=0),
            (((1,), (1,)), ((), ())),
            preferred_element_type=F32,
        )
        s = lax.broadcasted_iota(jnp.int32, (slots, 1), 0)
        same = lax.broadcasted_iota(jnp.int32, (slots, at), 1) // 8 == s // CAP
        rank = (s % CAP).astype(F32)
        for j in range(2):
            base = 2 * j * hidden
            gate = totals[:, base : base + hidden]
            up = totals[:, base + hidden : base + 2 * hidden]
            active = (gate / (1.0 + jnp.exp(-gate)) * up).astype(BF)
            pick = jnp.where(same & (held[j : j + 1, :] == rank), 1.0, 0.0).astype(BF)
            packed = jnp.dot(pick, active, preferred_element_type=F32)
            out_ref[:, j * hidden : (j + 1) * hidden] = packed.astype(BF)


def expert_slots(pieces, masks, weights):
    hidden, depth = weights[0].shape
    chunk = 1024
    steps = depth // chunk
    sizes = tuple(p.shape[0] for p in pieces)
    in_specs = [pl.BlockSpec((8, LANES), lambda k: (0, 0))]
    in_specs += [pl.BlockSpec((m, chunk), lambda k: (0, k)) for m in sizes]
    in_specs += [pl.BlockSpec((m, LANES), lambda k: (0, depth // LANES)) for m in sizes]
    in_specs += [pl.BlockSpec((hidden, chunk), lambda k: (0, k))] * 4
    in_hbm = lambda arrays: [pltpu.with_memory_space_constraint(a, pltpu.HBM) for a in arrays]
    pieces, weights = in_hbm(pieces), in_hbm(weights)
    total = sum(sizes)
    slots = total // 8 * CAP
    return pl.pallas_call(
        functools.partial(expert_kernel, sizes, steps),
        grid=(steps,),
        in_specs=in_specs,
        out_specs=pl.BlockSpec((slots, 2 * hidden), lambda k: (0, 0)),
        out_shape=jax.ShapeDtypeStruct((slots, 2 * hidden), BF),
        scratch_shapes=[
            pltpu.VMEM((total, chunk), BF),
            pltpu.VMEM((total, 4 * hidden), F32),
        ],
        compiler_params=pltpu.CompilerParams(vmem_limit_bytes=20 << 20),
        cost_estimate=pl.CostEstimate(
            flops=8 * total * depth * hidden,
            bytes_accessed=8 * depth * hidden + 2 * total * depth,
            transcendentals=2 * total * hidden,
        ),
        name="expert_slots",
    )(masks, *pieces, *pieces, *weights)


PIECES = (
    *((h, 0, i) for h in (0, 1) for i in (0, 2)),
    *((h, o, 0) for h in (0, 1) for o in (1, 3)),
    *((h, o, 2) for h in (0, 1) for o in (1, 3)),
    *((h, 2, i) for h in (0, 1) for i in (0, 2)),
)


def lower_kernel(place_ref, near_ref, own_ref, other_ref, *refs):
    members, hidden, _ = own_ref.shape
    rest_refs, (out_ref, *sums, placed) = refs[:members], refs[members:]
    first = near_ref.shape[1]
    z = place_ref[2]
    for j, w_ref in enumerate((own_ref, other_ref)):
        span = slice(j * hidden, (j + 1) * hidden)
        for d in range(members):
            at = (z + d) % members
            near = jnp.dot(near_ref[d][:, span], w_ref[d], preferred_element_type=F32)
            rest = jnp.dot(rest_refs[d][:, span], w_ref[at], preferred_element_type=F32)
            if d == 0:
                sums[j][:first, :] = near
                sums[j][first:, :] = rest
            else:
                sums[j][:first, :] += near
                sums[j][first:, :] += rest
    x, y = place_ref[0], place_ref[1]
    per = placed.shape[2] // 2
    for p, (h, outer, inner) in enumerate(PIECES):
        for i in range(2):
            at = (2 * p + i) * per
            if h == 0:
                chip = (x + inner + i) % 4 * 4 + (y + outer) % 4
            else:
                chip = (x + outer) % 4 * 4 + (y + inner + i) % 4
            for j in range(2):
                placed[chip, j, h * per : (h + 1) * per, :] = sums[j][at : at + per, :]
    out_ref[...] = placed[...].astype(BF)


def lower(place, near, rest, down_own, down_other, chips):
    members, hidden, cols = down_own.shape
    slots = near.shape[1] + rest[0].shape[0]
    per_chip = slots // chips
    return pl.pallas_call(
        lower_kernel,
        in_specs=[pl.BlockSpec(memory_space=pltpu.SMEM)]
        + [pl.BlockSpec(memory_space=pltpu.VMEM)] * (3 + members),
        out_specs=pl.BlockSpec(memory_space=pltpu.VMEM),
        out_shape=jax.ShapeDtypeStruct((chips, 2, per_chip, cols), BF),
        scratch_shapes=[
            pltpu.VMEM((slots, cols), F32),
            pltpu.VMEM((slots, cols), F32),
            pltpu.VMEM((chips, 2, per_chip, cols), F32),
        ],
        compiler_params=pltpu.CompilerParams(vmem_limit_bytes=16 << 20),
        cost_estimate=pl.CostEstimate(
            flops=4 * members * slots * hidden * cols,
            bytes_accessed=4 * members * hidden * (slots + cols),
            transcendentals=0,
        ),
        name="lower",
    )(place, near, down_own, down_other, *rest)


def attend_kernel(
    stream_ref, wq_ref, wk_ref, wv_ref, keys_ref, values_ref, start_ref, out_ref, normed, spread, own, fresh
):
    members, rows, cols = stream_ref.shape
    heads, size = out_ref.shape[1] // keys_ref.shape[2], keys_ref.shape[2]
    width = members * cols
    total = jnp.zeros((rows, 1), F32)
    for i in range(members):
        block = stream_ref[i].astype(F32)
        total += jnp.sum(block * block, axis=1, keepdims=True)
    scale = lax.rsqrt(total / width + EPSILON)
    for i in range(members):
        normed[:, i * cols : (i + 1) * cols] = (stream_ref[i].astype(F32) * scale).astype(BF)
    project = lambda w_ref: jnp.dot(normed[...], w_ref[...], preferred_element_type=F32)
    queries = project(wq_ref)
    key_new = project(wk_ref).astype(BF).astype(F32)
    value_new = project(wv_ref).astype(BF).astype(F32)
    pad = spread.shape[1] // 3
    factor = 1.0 / math.sqrt(size)
    for h in range(heads):
        query = queries[:, h * size : (h + 1) * size]
        for i, part in enumerate(split3(query)):
            spread[:, pad * i + h, :] = part.astype(F32)
        mine = jnp.sum(query * key_new, axis=1, keepdims=True) * factor
        own[:, h, :] = jnp.broadcast_to(mine, (rows, size))
        fresh[:, h, :] = value_new
    for h in range(heads, pad):
        for i in range(3):
            spread[:, pad * i + h, :] = jnp.zeros((rows, size), F32)
        own[:, h, :] = jnp.zeros((rows, size), F32)
        fresh[:, h, :] = jnp.zeros((rows, size), F32)

    def parts_dot(parts, cached, dim):
        result = lax.dot_general(
            parts.astype(BF), cached, (((2,), (dim,)), ((0,), (0,))), preferred_element_type=F32
        )
        return result[:, :pad] + result[:, pad : 2 * pad] + result[:, 2 * pad :]

    scores = parts_dot(spread[...], keys_ref[...], 2) * factor
    window = scores.shape[2]
    allowed = lax.broadcasted_iota(jnp.int32, scores.shape, 2) >= start_ref[...]
    masked = jnp.where(allowed, scores, -jnp.inf)
    own_score = own[...]
    highest = jnp.maximum(jnp.max(masked, axis=2, keepdims=True), own_score[:, :, :1])
    weights = jnp.exp(masked - highest)
    own_weight = jnp.exp(own_score - highest)
    denominator = jnp.sum(weights, axis=2, keepdims=True) + own_weight[:, :, :1]
    probabilities = weights / denominator
    split = jnp.concatenate([part.astype(F32) for part in split3(probabilities)], axis=1)
    attended = parts_dot(split, values_ref[...], 1) + own_weight / denominator * fresh[...]
    own[...] = attended
    for h in range(heads):
        out_ref[:, h * size : (h + 1) * size] = own[:, h, :].astype(BF)


def attend(group_stream, w_query, w_key, w_value, cache_keys, cache_values, lengths):
    members, rows, cols = group_stream.shape
    window, size = cache_keys.shape[2:]
    pad = 8
    start = jnp.broadcast_to((window - lengths)[:, None, None], (rows, pad, window))
    return pl.pallas_call(
        attend_kernel,
        in_specs=[pl.BlockSpec(memory_space=pltpu.VMEM)] * 7,
        out_specs=pl.BlockSpec(memory_space=pltpu.VMEM),
        out_shape=jax.ShapeDtypeStruct((rows, w_query.shape[1]), BF),
        scratch_shapes=[
            pltpu.VMEM((rows, members * cols), BF),
            pltpu.VMEM((rows, 3 * pad, size), F32),
            pltpu.VMEM((rows, pad, size), F32),
            pltpu.VMEM((rows, pad, size), F32),
        ],
        compiler_params=pltpu.CompilerParams(vmem_limit_bytes=24 << 20),
        cost_estimate=pl.CostEstimate(
            flops=2 * rows * members * cols * (w_query.shape[1] + 2 * size),
            bytes_accessed=2 * members * cols * (w_query.shape[1] + 2 * size),
            transcendentals=rows * pad * window,
        ),
        name="attend",
    )(
        group_stream,
        w_query,
        w_key,
        w_value,
        cache_keys[:, 0],
        cache_values[:, 0],
        start.astype(jnp.int32),
    )


def split3(values):
    high = values.astype(BF)
    rest = values - high.astype(F32)
    middle = rest.astype(BF)
    return high, middle, (rest - middle.astype(F32)).astype(BF)


def routing_columns(expert_ids, combine, experts):
    named = expert_ids[:, :, None] == jnp.arange(experts, dtype=jnp.int32)
    chosen = jnp.any(named, axis=1)
    weight = jnp.sum(jnp.where(named, combine[:, :, None], 0.0), axis=1)
    rows = jnp.arange(expert_ids.shape[0])
    earlier = rows[None, :, None] < rows[:, None, None]
    rank = jnp.sum((earlier & chosen[None]).astype(jnp.int32), axis=1)
    rank = jnp.where(chosen, rank, CAP).astype(BF)
    return jnp.concatenate([rank, *split3(weight)], axis=1)


def per_device(
    tokens,
    expert_ids,
    combine,
    w_gate,
    w_up,
    w_down,
    w_query,
    w_key,
    w_value,
    cache_keys,
    cache_values,
    lengths,
):
    rows_n, width = tokens.shape
    x, y, c, z = (lax.axis_index(a) for a in ("x", "y", "c", "z"))
    chips = lax.axis_size("x") * lax.axis_size("y")
    experts = 2 * chips
    members = lax.axis_size("z")
    group = rows_n * members
    hidden = w_gate.shape[2]
    cols = width // members

    sent = jnp.concatenate([tokens, routing_columns(expert_ids, combine, experts)], axis=1)
    own = [w_gate[0].T, w_up[0].T]
    arrived, *other = lax.optimization_barrier(
        (copies(sent, "z"), *(shift(w, "c", 1) for w in own))
    )
    weights = own + other
    arrived = arrived.reshape(group, width + LANES)
    group_tokens, meta = arrived[:, :width], arrived[:, width:]
    widened = group_tokens.astype(F32)
    normed = (
        widened * lax.rsqrt(jnp.mean(widened * widened, axis=-1, keepdims=True) + EPSILON)
    ).astype(BF)
    dense = jnp.concatenate([normed, meta], axis=1)

    lane = jnp.arange(LANES, dtype=jnp.int32)[None, :]
    e_own = (x * 4 + y) * 2 + c
    e_other = (x * 4 + y) * 2 + 1 - c
    masks = jnp.concatenate([lane == e_own, lane == e_other] + [lane < 0] * 6, axis=0).astype(F32)
    masks = masks.astype(BF)
    half = group // 2

    def first_ring(block, axis):
        after, before, opposite = (shift(block, axis, step) for step in (1, -1, 2))
        return (
            jnp.concatenate([block, after], axis=0),
            jnp.concatenate([opposite, before], axis=0),
        )

    a_near, a_far = first_ring(dense[:half], "x")
    b_near, b_far = first_ring(dense[half:], "y")
    a_far, b_far, down = lax.optimization_barrier((a_far, b_far, w_down[0]))
    down_own = lax.all_to_all(down, "z", 1, 0, tiled=True).reshape(members, hidden, cols)
    sides = lambda part, axis: (shift(part, axis, 1), shift(part, axis, -1))
    a_near_sides, b_near_sides = sides(a_near, "y"), sides(b_near, "x")
    a_far_sides, b_far_sides = sides(a_far, "y"), sides(b_far, "x")
    near = (a_near, a_far, b_near, b_far, *a_near_sides, *b_near_sides)
    far = (*a_far_sides, *b_far_sides)
    slots = expert_slots(near, masks, weights)
    slots, *far = lax.optimization_barrier((slots, *far))
    opposite = (
        shift(a_near_sides[1], "y", -1),
        shift(far[0], "y", 1),
        shift(b_near_sides[1], "x", -1),
        shift(far[2], "x", 1),
    )
    near_active = lax.all_gather(slots, "z", axis=0)
    more, down_own = lax.optimization_barrier((expert_slots(far, masks, weights), down_own))
    down_other = shift(down_own, "c", 1)
    rest = jnp.concatenate([more, expert_slots(opposite, masks, weights)], axis=0)
    active = (near_active, ring(rest, "z"))
    place = jnp.stack([x, y, z]).astype(jnp.int32)
    result = lower(place, *active, down_own, down_other, chips)
    per_chip = result.shape[2]
    result = result.reshape(chips, 2 * per_chip, cols)
    returned = lax.all_to_all(result, ("x", "y"), 0, 0, tiled=True)

    rank = meta[:, :experts].astype(F32)
    weight = sum(meta[:, i * experts : (i + 1) * experts].astype(F32) for i in (1, 2, 3))
    by_core = lambda v: v.reshape(group, chips, 2)
    order = lambda v: jnp.where(c == 0, by_core(v), by_core(v)[:, :, ::-1])
    rank, weight = order(rank), order(weight)
    slot = jnp.arange(per_chip, dtype=jnp.int32)
    mine = (slot // CAP)[None, :] == (jnp.arange(group) // rows_n)[:, None]
    hit = mine[:, None, None, :] & (
        rank[..., None] == (slot % CAP).astype(F32)[None, None, None, :]
    )
    spread = jnp.where(hit, weight[..., None], 0.0).reshape(group, chips * 2 * per_chip)
    mixture = jnp.dot(
        spread,
        returned.reshape(chips * 2 * per_chip, cols).astype(F32),
        precision=lax.Precision.HIGHEST,
        preferred_element_type=F32,
    )
    block_tokens = lax.dynamic_slice(group_tokens, (jnp.int32(0), z * cols), (group, cols))
    stream_block = (block_tokens.astype(F32) + mixture).astype(BF)
    group_stream = copies(stream_block, "z")
    stream = lax.dynamic_slice(
        group_stream, (jnp.int32(0), z * rows_n, jnp.int32(0)), (members, rows_n, cols)
    )
    stream = stream.transpose(1, 0, 2).reshape(rows_n, width)
    guard = attend(group_stream, w_query, w_key, w_value, cache_keys, cache_values, lengths)
    return (stream, guard)


def solution(mesh):
    torus = Mesh(mesh.devices.reshape(4, 4, 2, mesh.devices.shape[1]), ("x", "y", "c", "z"))
    ep = ("x", "y", "c")
    every = (*ep, "z")
    return jax.shard_map(
        per_device,
        mesh=torus,
        in_specs=(
            P(every, None),
            P(every, None),
            P(every, None),
            P(ep, None, "z"),
            P(ep, None, "z"),
            P(ep, "z", None),
            P(None, "z"),
            P(None, "z"),
            P(None, "z"),
            P(ep, "z", None, None),
            P(ep, "z", None, None),
            P(ep),
        ),
        out_specs=(P(every, None), P(ep, "z")),
        check_vma=False,
    )
```

```python
import functools
import math

import jax
import jax.numpy as jnp
from jax import lax
from jax.experimental import pallas as pl
from jax.experimental.pallas import tpu as pltpu
from jax.sharding import Mesh
from jax.sharding import PartitionSpec as P

EPSILON = 1e-06
BF = jnp.bfloat16
F32 = jnp.float32
LANES = 128
CAP = 3


def shift(values, axis, step):
    size = lax.axis_size(axis)
    return lax.ppermute(values, axis, [(i, (i - step) % size) for i in range(size)])


def ring(block, axis):
    size = lax.axis_size(axis)
    pieces = [block] + [None] * (size - 1)
    after = before = block
    for d in range(1, size // 2):
        after, before = shift(after, axis, 1), shift(before, axis, -1)
        pieces[d], pieces[size - d] = after, before
    mid = block.shape[0] // 2
    farthest = shift(after[:mid], axis, 1), shift(before[mid:], axis, -1)
    pieces[size // 2] = jnp.concatenate(farthest, axis=0)
    return pieces


def copies(values, axis):
    size = lax.axis_size(axis)
    return lax.all_to_all(
        jnp.broadcast_to(values[None], (size, *values.shape)), axis, 0, 0, tiled=True
    )


def in_hbm(arrays):
    return [pltpu.with_memory_space_constraint(a, pltpu.HBM) for a in arrays]


def expert_kernel(sizes, steps, mask_ref, *refs):
    n = len(sizes)
    rows, meta = refs[:n], refs[n : 2 * n]
    w_refs = refs[2 * n : 2 * n + 4]
    out_ref, joined, totals = refs[2 * n + 4 :]
    k = pl.program_id(0)
    hidden = w_refs[0].shape[0]
    at = 0
    for m, row_ref in zip(sizes, rows):
        joined[at : at + m, :] = row_ref[...]
        at += m
    part = lax.dot_general(
        joined[...],
        jnp.concatenate([w_ref[...] for w_ref in w_refs], axis=0),
        (((1,), (1,)), ((), ())),
        preferred_element_type=F32,
    )

    @pl.when(k == 0)
    def _():
        totals[...] = part

    @pl.when(k > 0)
    def _():
        totals[...] += part

    @pl.when(k == steps - 1)
    def _():
        slots = out_ref.shape[0]
        held = lax.dot_general(
            mask_ref[...],
            jnp.concatenate([m_ref[...] for m_ref in meta], axis=0),
            (((1,), (1,)), ((), ())),
            preferred_element_type=F32,
        )
        s = lax.broadcasted_iota(jnp.int32, (slots, 1), 0)
        same = lax.broadcasted_iota(jnp.int32, (slots, at), 1) // 8 == s // CAP
        rank = (s % CAP).astype(F32)
        for j in range(2):
            base = 2 * j * hidden
            gate = totals[:, base : base + hidden]
            up = totals[:, base + hidden : base + 2 * hidden]
            active = (gate / (1.0 + jnp.exp(-gate)) * up).astype(BF)
            pick = jnp.where(same & (held[j : j + 1, :] == rank), 1.0, 0.0).astype(BF)
            packed = jnp.dot(pick, active, preferred_element_type=F32)
            out_ref[:, j * hidden : (j + 1) * hidden] = packed.astype(BF)


def expert_slots(pieces, masks, weights):
    hidden, depth = weights[0].shape
    chunk = 1024
    steps = depth // chunk
    sizes = tuple(p.shape[0] for p in pieces)
    in_specs = [pl.BlockSpec((8, LANES), lambda k: (0, 0))]
    in_specs += [pl.BlockSpec((m, chunk), lambda k: (0, k)) for m in sizes]
    in_specs += [pl.BlockSpec((m, LANES), lambda k: (0, depth // LANES)) for m in sizes]
    in_specs += [pl.BlockSpec((hidden, chunk), lambda k: (0, k))] * 4
    pieces, weights = in_hbm(pieces), in_hbm(weights)
    total = sum(sizes)
    slots = total // 8 * CAP
    return pl.pallas_call(
        functools.partial(expert_kernel, sizes, steps),
        grid=(steps,),
        in_specs=in_specs,
        out_specs=pl.BlockSpec((slots, 2 * hidden), lambda k: (0, 0)),
        out_shape=jax.ShapeDtypeStruct((slots, 2 * hidden), BF),
        scratch_shapes=[
            pltpu.VMEM((total, chunk), BF),
            pltpu.VMEM((total, 4 * hidden), F32),
        ],
        compiler_params=pltpu.CompilerParams(vmem_limit_bytes=20 << 20),
        cost_estimate=pl.CostEstimate(
            flops=8 * total * depth * hidden,
            bytes_accessed=8 * depth * hidden + 2 * total * depth,
            transcendentals=2 * total * hidden,
        ),
        name="expert_slots",
    )(masks, *pieces, *pieces, *weights)


PIECES = (
    *((h, 0, i) for h in (0, 1) for i in (0, 2)),
    *((h, o, 0) for h in (0, 1) for o in (1, 3)),
    *((h, o, 2) for h in (0, 1) for o in (1, 3)),
    *((h, 2, i) for h in (0, 1) for i in (0, 2)),
)


def lower_kernel(place_ref, near_ref, own_ref, other_ref, *refs):
    members, hidden, _ = own_ref.shape
    rest_refs, refs = refs[:members], refs[members:]
    out_ref, first_sum, second_sum, placed, near_held, own_held, other_held, sems = refs
    sums = (first_sum, second_sum)
    first = near_ref.shape[1]
    z = place_ref[2]

    def copy(i, d):
        source, target = ((near_ref, near_held), (own_ref, own_held), (other_ref, other_held))[i]
        return pltpu.make_async_copy(source.at[d], target.at[d], sems.at[i, d])

    for d in range(members):
        for i in range(3):
            copy(i, d).start()
    for d in range(members):
        for i in range(3):
            copy(i, d).wait()
        for j, held in enumerate((own_held, other_held)):
            span = slice(j * hidden, (j + 1) * hidden)
            part = jnp.dot(near_held[d][:, span], held[d], preferred_element_type=F32)
            if d == 0:
                sums[j][:first, :] = part
            else:
                sums[j][:first, :] += part
    for j, held in enumerate((own_held, other_held)):
        span = slice(j * hidden, (j + 1) * hidden)
        for d in range(members):
            at = (z + d) % members
            part = jnp.dot(rest_refs[d][:, span], held[at], preferred_element_type=F32)
            if d == 0:
                sums[j][first:, :] = part
            else:
                sums[j][first:, :] += part
    x, y = place_ref[0], place_ref[1]
    per = placed.shape[2] // 2
    for p, (h, outer, inner) in enumerate(PIECES):
        for i in range(2):
            at = (2 * p + i) * per
            step = (0, 1, 3, 2)[inner + i]
            if h == 0:
                chip = (x ^ step) * 4 + (y + outer) % 4
            else:
                chip = (x + outer) % 4 * 4 + (y ^ step)
            for j in range(2):
                placed[chip, j, h * per : (h + 1) * per, :] = sums[j][at : at + per, :]
    out_ref[...] = placed[...].astype(BF)


def lower(place, near, rest, down_own, down_other, chips):
    members, hidden, cols = down_own.shape
    near, down_own, down_other = in_hbm((near, down_own, down_other))
    slots = near.shape[1] + rest[0].shape[0]
    per_chip = slots // chips
    return pl.pallas_call(
        lower_kernel,
        in_specs=[pl.BlockSpec(memory_space=pltpu.SMEM)]
        + [pl.BlockSpec(memory_space=pl.ANY)] * 3
        + [pl.BlockSpec(memory_space=pltpu.VMEM)] * members,
        out_specs=pl.BlockSpec(memory_space=pltpu.VMEM),
        out_shape=jax.ShapeDtypeStruct((chips, 2, per_chip, cols), BF),
        scratch_shapes=[
            pltpu.VMEM((slots, cols), F32),
            pltpu.VMEM((slots, cols), F32),
            pltpu.VMEM((chips, 2, per_chip, cols), F32),
            pltpu.VMEM(near.shape, BF),
            pltpu.VMEM(down_own.shape, BF),
            pltpu.VMEM(down_other.shape, BF),
            pltpu.SemaphoreType.DMA((3, members)),
        ],
        compiler_params=pltpu.CompilerParams(vmem_limit_bytes=24 << 20),
        cost_estimate=pl.CostEstimate(
            flops=4 * members * slots * hidden * cols,
            bytes_accessed=4 * members * hidden * (slots + cols),
            transcendentals=0,
        ),
        name="lower",
    )(place, near, down_own, down_other, *rest)


def attend_kernel(
    place_ref, stream_ref, wq_ref, wk_ref, wv_ref, keys_ref, values_ref, start_ref, mine_ref, out_ref, *scratch
):
    normed, spread, own, fresh, wide, *held, sems, query_sems = scratch
    sources = (wk_ref, wv_ref, keys_ref, values_ref)
    moves = [pltpu.make_async_copy(s, t, sems.at[i]) for i, (s, t) in enumerate(zip(sources, held[1:]))]
    members, rows, cols = stream_ref.shape
    parts = [pl.ds(i * cols, cols) for i in range(members)]
    query_moves = [
        pltpu.make_async_copy(wq_ref.at[p], held[0].at[p], query_sems.at[i]) for i, p in enumerate(parts)
    ]
    for move in (*query_moves, *moves):
        move.start()
    members, rows, cols = stream_ref.shape
    heads, size = out_ref.shape[1] // keys_ref.shape[2], keys_ref.shape[2]
    width = members * cols
    total = jnp.zeros((rows, 1), F32)
    for i in range(members):
        block = stream_ref[i].astype(F32)
        wide[...] = block
        few = mine_ref.shape[0]
        mine = wide[pl.ds(pl.multiple_of(place_ref[2] * few, few), few), :]
        mine_ref[:, i * cols : (i + 1) * cols] = mine.astype(BF)
        total += jnp.sum(block * block, axis=1, keepdims=True)
    scale = lax.rsqrt(total / width + EPSILON)
    for i in range(members):
        normed[:, i * cols : (i + 1) * cols] = (stream_ref[i].astype(F32) * scale).astype(BF)
    queries = jnp.zeros((rows, out_ref.shape[1]), F32)
    for move, p in zip(query_moves, parts):
        move.wait()
        queries += jnp.dot(normed[:, p], held[0][p, :], preferred_element_type=F32)

    def project(i):
        moves[i].wait()
        return jnp.dot(normed[...], held[1 + i][...], preferred_element_type=F32)

    key_new = project(0).astype(BF).astype(F32)
    value_new = project(1).astype(BF).astype(F32)
    pad = spread.shape[1] // 3
    factor = 1.0 / math.sqrt(size)
    for h in range(heads):
        query = queries[:, h * size : (h + 1) * size]
        for i, part in enumerate(split3(query)):
            spread[:, pad * i + h, :] = part.astype(F32)
        mine = jnp.sum(query * key_new, axis=1, keepdims=True) * factor
        own[:, h, :] = jnp.broadcast_to(mine, (rows, size))
        fresh[:, h, :] = value_new
    for h in range(heads, pad):
        for i in range(3):
            spread[:, pad * i + h, :] = jnp.zeros((rows, size), F32)
        own[:, h, :] = jnp.zeros((rows, size), F32)
        fresh[:, h, :] = jnp.zeros((rows, size), F32)

    def parts_dot(parts, cached, dim):
        result = lax.dot_general(
            parts.astype(BF), cached, (((2,), (dim,)), ((0,), (0,))), preferred_element_type=F32
        )
        return result[:, :pad] + result[:, pad : 2 * pad] + result[:, 2 * pad :]

    moves[2].wait()
    scores = parts_dot(spread[...], held[3][...], 2) * factor
    window = scores.shape[2]
    allowed = lax.broadcasted_iota(jnp.int32, scores.shape, 2) >= start_ref[...]
    masked = jnp.where(allowed, scores, -jnp.inf)
    own_score = own[...]
    highest = jnp.maximum(jnp.max(masked, axis=2, keepdims=True), own_score[:, :, :1])
    weights = jnp.exp(masked - highest)
    own_weight = jnp.exp(own_score - highest)
    denominator = jnp.sum(weights, axis=2, keepdims=True) + own_weight[:, :, :1]
    probabilities = weights / denominator
    split = jnp.concatenate([part.astype(F32) for part in split3(probabilities)], axis=1)
    moves[3].wait()
    attended = parts_dot(split, held[4][...], 1) + own_weight / denominator * fresh[...]
    own[...] = attended
    for h in range(heads):
        out_ref[:, h * size : (h + 1) * size] = own[:, h, :].astype(BF)


def attend(place, group_stream, w_query, w_key, w_value, cache_keys, cache_values, lengths):
    members, rows, cols = group_stream.shape
    window, size = cache_keys.shape[1:]
    pad = 8
    large = in_hbm((w_query, w_key, w_value, cache_keys, cache_values))
    start = jnp.broadcast_to((window - lengths)[:, None, None], (rows, pad, window))
    return pl.pallas_call(
        attend_kernel,
        in_specs=[pl.BlockSpec(memory_space=pltpu.SMEM), pl.BlockSpec(memory_space=pltpu.VMEM)]
        + [pl.BlockSpec(memory_space=pl.ANY)] * 5
        + [pl.BlockSpec(memory_space=pltpu.VMEM)],
        out_specs=[pl.BlockSpec(memory_space=pltpu.VMEM)] * 2,
        out_shape=[
            jax.ShapeDtypeStruct((rows // members, members * cols), BF),
            jax.ShapeDtypeStruct((rows, w_query.shape[1]), BF),
        ],
        scratch_shapes=[
            pltpu.VMEM((rows, members * cols), BF),
            pltpu.VMEM((rows, 3 * pad, size), F32),
            pltpu.VMEM((rows, pad, size), F32),
            pltpu.VMEM((rows, pad, size), F32),
            pltpu.VMEM((rows, cols), F32),
            *(pltpu.VMEM(a.shape, a.dtype) for a in large),
            pltpu.SemaphoreType.DMA((4,)),
            pltpu.SemaphoreType.DMA((members,)),
        ],
        compiler_params=pltpu.CompilerParams(vmem_limit_bytes=24 << 20),
        cost_estimate=pl.CostEstimate(
            flops=2 * rows * members * cols * (w_query.shape[1] + 2 * size),
            bytes_accessed=2 * members * cols * (w_query.shape[1] + 2 * size),
            transcendentals=rows * pad * window,
        ),
        name="attend",
    )(
        place,
        group_stream,
        *large,
        start.astype(jnp.int32),
    )


def split3(values):
    high = values.astype(BF)
    rest = values - high.astype(F32)
    middle = rest.astype(BF)
    return high, middle, (rest - middle.astype(F32)).astype(BF)


def routing_columns(expert_ids, combine, experts):
    named = expert_ids[:, :, None] == jnp.arange(experts, dtype=jnp.int32)
    chosen = jnp.any(named, axis=1)
    weight = jnp.sum(jnp.where(named, combine[:, :, None], 0.0), axis=1)
    rows = jnp.arange(expert_ids.shape[0])
    earlier = rows[None, :, None] < rows[:, None, None]
    rank = jnp.sum((earlier & chosen[None]).astype(jnp.int32), axis=1)
    rank = jnp.where(chosen, rank, CAP).astype(BF)
    return jnp.concatenate([rank, *split3(weight)], axis=1)


def per_device(
    tokens,
    expert_ids,
    combine,
    w_gate,
    w_up,
    w_down,
    w_query,
    w_key,
    w_value,
    cache_keys,
    cache_values,
    lengths,
):
    rows_n, width = tokens.shape
    x, y, c, z = (lax.axis_index(a) for a in ("x", "y", "c", "z"))
    chips = lax.axis_size("x") * lax.axis_size("y")
    experts = 2 * chips
    members = lax.axis_size("z")
    group = rows_n * members
    hidden = w_gate.shape[2]
    cols = width // members

    sent = jnp.concatenate([tokens, routing_columns(expert_ids, combine, experts)], axis=1)
    own = [w_gate[0].T, w_up[0].T]
    arrived, down, *other = lax.optimization_barrier(
        (copies(sent, "z"), w_down[0], *(shift(w, "c", 1) for w in own))
    )
    weights = own + other
    down_own = lax.all_to_all(down, "z", 1, 0, tiled=True).reshape(members, hidden, cols)
    arrived = arrived.reshape(group, width + LANES)
    group_tokens, meta = arrived[:, :width], arrived[:, width:]
    widened = group_tokens.astype(F32)
    normed = (
        widened * lax.rsqrt(jnp.mean(widened * widened, axis=-1, keepdims=True) + EPSILON)
    ).astype(BF)
    dense = jnp.concatenate([normed, meta], axis=1)

    lane = jnp.arange(LANES, dtype=jnp.int32)[None, :]
    e_own = (x * 4 + y) * 2 + c
    e_other = (x * 4 + y) * 2 + 1 - c
    masks = jnp.concatenate([lane == e_own, lane == e_other] + [lane < 0] * 6, axis=0).astype(F32)
    masks = masks.astype(BF)
    half = group // 2

    def pairs(block, axis, mask):
        return lax.ppermute(block, axis, [(i, i ^ mask) for i in range(4)])

    def near_rows(block, axis):
        return jnp.concatenate([block, pairs(block, axis, 1)], axis=0)

    sides = lambda part, axis: (shift(part, axis, 1), shift(part, axis, -1))
    a_near, b_near = near_rows(dense[:half], "x"), near_rows(dense[half:], "y")
    a_far, b_far = pairs(a_near, "x", 3), pairs(b_near, "y", 3)
    a_near_sides, b_near_sides = sides(a_near, "y"), sides(b_near, "x")
    a_far_sides, b_far_sides = sides(a_far, "y"), sides(b_far, "x")
    near = (a_near, a_far, b_near, b_far, *a_near_sides, *b_near_sides)
    far = (*a_far_sides, *b_far_sides)
    slots = expert_slots(near, masks, weights)
    slots, *far = lax.optimization_barrier((slots, *far))
    opposite = (
        shift(a_near_sides[1], "y", -1),
        shift(far[0], "y", 1),
        shift(b_near_sides[1], "x", -1),
        shift(far[2], "x", 1),
    )
    near_active = lax.all_gather(slots, "z", axis=0)
    more, down_own = lax.optimization_barrier((expert_slots(far, masks, weights), down_own))
    down_other = shift(down_own, "c", 1)
    rest = jnp.concatenate([more, expert_slots(opposite, masks, weights)], axis=0)
    active = (near_active, ring(rest, "z"))
    place = jnp.stack([x, y, z]).astype(jnp.int32)
    result = lower(place, *active, down_own, down_other, chips)
    per_chip = result.shape[2]
    result = result.reshape(chips, 2 * per_chip, cols)
    returned = lax.all_to_all(result, ("x", "y"), 0, 0, tiled=True)

    rank = meta[:, :experts].astype(F32)
    weight = sum(meta[:, i * experts : (i + 1) * experts].astype(F32) for i in (1, 2, 3))
    by_core = lambda v: v.reshape(group, chips, 2)
    order = lambda v: jnp.where(c == 0, by_core(v), by_core(v)[:, :, ::-1])
    rank, weight = order(rank), order(weight)
    slot = jnp.arange(per_chip, dtype=jnp.int32)
    mine = (slot // CAP)[None, :] == (jnp.arange(group) // rows_n)[:, None]
    hit = mine[:, None, None, :] & (
        rank[..., None] == (slot % CAP).astype(F32)[None, None, None, :]
    )
    spread = jnp.where(hit, weight[..., None], 0.0).reshape(group, chips * 2 * per_chip)
    mixture = jnp.dot(
        spread,
        returned.reshape(chips * 2 * per_chip, cols).astype(F32),
        precision=lax.Precision.HIGHEST,
        preferred_element_type=F32,
    )
    block_tokens = lax.dynamic_slice(group_tokens, (jnp.int32(0), z * cols), (group, cols))
    stream_block = (block_tokens.astype(F32) + mixture).astype(BF)
    guard_args = (w_query, w_key, w_value, cache_keys[:, 0], cache_values[:, 0])
    group_stream = copies(stream_block, "z")
    stream, guard = attend(place, group_stream, *guard_args, lengths)
    return (stream, guard)


def solution(mesh):
    torus = Mesh(mesh.devices.reshape(4, 4, 2, mesh.devices.shape[1]), ("x", "y", "c", "z"))
    ep = ("x", "y", "c")
    every = (*ep, "z")
    return jax.shard_map(
        per_device,
        mesh=torus,
        in_specs=(
            P(every, None),
            P(every, None),
            P(every, None),
            P(ep, None, "z"),
            P(ep, None, "z"),
            P(ep, "z", None),
            P(None, "z"),
            P(None, "z"),
            P(None, "z"),
            P(ep, "z", None, None),
            P(ep, "z", None, None),
            P(ep),
        ),
        out_specs=(P(every, None), P(ep, "z")),
        check_vma=False,
    )
```

```python
import functools
import math

import jax
import jax.numpy as jnp
from jax import lax
from jax.experimental import pallas as pl
from jax.experimental.pallas import tpu as pltpu
from jax.sharding import Mesh
from jax.sharding import PartitionSpec as P

EPSILON = 1e-06
BF = jnp.bfloat16
F32 = jnp.float32
LANES = 128
CAP = 3


def shift(values, axis, step):
    size = lax.axis_size(axis)
    return lax.ppermute(values, axis, [(i, (i - step) % size) for i in range(size)])


def ring(block, axis):
    size = lax.axis_size(axis)
    pieces = [block] + [None] * (size - 1)
    after = before = block
    for d in range(1, size // 2):
        after, before = shift(after, axis, 1), shift(before, axis, -1)
        pieces[d], pieces[size - d] = after, before
    mid = block.shape[0] // 2
    farthest = shift(after[:mid], axis, 1), shift(before[mid:], axis, -1)
    pieces[size // 2] = jnp.concatenate(farthest, axis=0)
    return pieces


def copies(values, axis):
    size = lax.axis_size(axis)
    return lax.all_to_all(
        jnp.broadcast_to(values[None], (size, *values.shape)), axis, 0, 0, tiled=True
    )


def in_hbm(arrays):
    return [pltpu.with_memory_space_constraint(a, pltpu.HBM) for a in arrays]


def expert_kernel(sizes, steps, mask_ref, *refs):
    n = len(sizes)
    rows, meta = refs[:n], refs[n : 2 * n]
    w_refs = refs[2 * n : 2 * n + 4]
    out_ref, joined, totals = refs[2 * n + 4 :]
    k = pl.program_id(0)
    hidden = w_refs[0].shape[0]
    at = 0
    for m, row_ref in zip(sizes, rows):
        joined[at : at + m, :] = row_ref[...]
        at += m
    part = lax.dot_general(
        joined[...],
        jnp.concatenate([w_ref[...] for w_ref in w_refs], axis=0),
        (((1,), (1,)), ((), ())),
        preferred_element_type=F32,
    )

    @pl.when(k == 0)
    def _():
        totals[...] = part

    @pl.when(k > 0)
    def _():
        totals[...] += part

    @pl.when(k == steps - 1)
    def _():
        slots = out_ref.shape[0]
        held = lax.dot_general(
            mask_ref[...],
            jnp.concatenate([m_ref[...] for m_ref in meta], axis=0),
            (((1,), (1,)), ((), ())),
            preferred_element_type=F32,
        )
        s = lax.broadcasted_iota(jnp.int32, (slots, 1), 0)
        same = lax.broadcasted_iota(jnp.int32, (slots, at), 1) // 8 == s // CAP
        rank = (s % CAP).astype(F32)
        for j in range(2):
            base = 2 * j * hidden
            gate = totals[:, base : base + hidden]
            up = totals[:, base + hidden : base + 2 * hidden]
            active = (gate / (1.0 + jnp.exp(-gate)) * up).astype(BF)
            pick = jnp.where(same & (held[j : j + 1, :] == rank), 1.0, 0.0).astype(BF)
            packed = jnp.dot(pick, active, preferred_element_type=F32)
            out_ref[:, j * hidden : (j + 1) * hidden] = packed.astype(BF)


def expert_slots(pieces, masks, weights):
    hidden, depth = weights[0].shape
    chunk = 1024
    steps = depth // chunk
    sizes = tuple(p.shape[0] for p in pieces)
    in_specs = [pl.BlockSpec((8, LANES), lambda k: (0, 0))]
    in_specs += [pl.BlockSpec((m, chunk), lambda k: (0, k)) for m in sizes]
    in_specs += [pl.BlockSpec((m, LANES), lambda k: (0, depth // LANES)) for m in sizes]
    in_specs += [pl.BlockSpec((hidden, chunk), lambda k: (0, k))] * 4
    pieces, weights = in_hbm(pieces), in_hbm(weights)
    total = sum(sizes)
    slots = total // 8 * CAP
    return pl.pallas_call(
        functools.partial(expert_kernel, sizes, steps),
        grid=(steps,),
        in_specs=in_specs,
        out_specs=pl.BlockSpec((slots, 2 * hidden), lambda k: (0, 0)),
        out_shape=jax.ShapeDtypeStruct((slots, 2 * hidden), BF),
        scratch_shapes=[
            pltpu.VMEM((total, chunk), BF),
            pltpu.VMEM((total, 4 * hidden), F32),
        ],
        compiler_params=pltpu.CompilerParams(vmem_limit_bytes=20 << 20),
        cost_estimate=pl.CostEstimate(
            flops=8 * total * depth * hidden,
            bytes_accessed=8 * depth * hidden + 2 * total * depth,
            transcendentals=2 * total * hidden,
        ),
        name="expert_slots",
    )(masks, *pieces, *pieces, *weights)


PIECES = (
    *((h, 0, i) for h in (0, 1) for i in (0, 2)),
    *((h, o, 0) for h in (0, 1) for o in (1, 3)),
    *((h, o, 2) for h in (0, 1) for o in (1, 3)),
    *((h, 2, i) for h in (0, 1) for i in (0, 2)),
)


def lower_kernel(place_ref, own_ref, other_ref, *refs):
    members, hidden, _ = own_ref.shape
    active_refs, refs = refs[:members], refs[members:]
    out_ref, first_sum, second_sum, placed, own_held, other_held, sems = refs
    sums = (first_sum, second_sum)
    pairs = ((own_ref, own_held), (other_ref, other_held))
    z = place_ref[2]
    moves = []
    for d in range(members):
        at = (z + d) % members
        moves.append(
            [pltpu.make_async_copy(s.at[at], t.at[d], sems.at[i, d]) for i, (s, t) in enumerate(pairs)]
        )
        for move in moves[d]:
            move.start()
    for d in range(members):
        for j, held in enumerate((own_held, other_held)):
            moves[d][j].wait()
            span = slice(j * hidden, (j + 1) * hidden)
            part = jnp.dot(active_refs[d][:, span], held[d], preferred_element_type=F32)
            if d == 0:
                sums[j][...] = part
            else:
                sums[j][...] += part
    x, y = place_ref[0], place_ref[1]
    per = placed.shape[2] // 2
    for p, (h, outer, inner) in enumerate(PIECES):
        for i in range(2):
            at = (2 * p + i) * per
            step = (0, 1, 3, 2)[inner + i]
            if h == 0:
                chip = (x ^ step) * 4 + (y + outer) % 4
            else:
                chip = (x + outer) % 4 * 4 + (y ^ step)
            for j in range(2):
                placed[chip, j, h * per : (h + 1) * per, :] = sums[j][at : at + per, :]
    out_ref[...] = placed[...].astype(BF)


def lower(place, active, down_own, down_other, chips):
    members, hidden, cols = down_own.shape
    down_own, down_other = in_hbm((down_own, down_other))
    slots = active[0].shape[0]
    per_chip = slots // chips
    return pl.pallas_call(
        lower_kernel,
        in_specs=[pl.BlockSpec(memory_space=pltpu.SMEM)]
        + [pl.BlockSpec(memory_space=pl.ANY)] * 2
        + [pl.BlockSpec(memory_space=pltpu.VMEM)] * members,
        out_specs=pl.BlockSpec(memory_space=pltpu.VMEM),
        out_shape=jax.ShapeDtypeStruct((chips, 2, per_chip, cols), BF),
        scratch_shapes=[
            pltpu.VMEM((slots, cols), F32),
            pltpu.VMEM((slots, cols), F32),
            pltpu.VMEM((chips, 2, per_chip, cols), F32),
            pltpu.VMEM(down_own.shape, BF),
            pltpu.VMEM(down_other.shape, BF),
            pltpu.SemaphoreType.DMA((2, members)),
        ],
        compiler_params=pltpu.CompilerParams(vmem_limit_bytes=24 << 20),
        cost_estimate=pl.CostEstimate(
            flops=4 * members * slots * hidden * cols,
            bytes_accessed=4 * members * hidden * (slots + cols),
            transcendentals=0,
        ),
        name="lower",
    )(place, down_own, down_other, *active)


def attend_kernel(
    place_ref, stream_ref, wq_ref, wk_ref, wv_ref, keys_ref, values_ref, start_ref, mine_ref, out_ref, *scratch
):
    normed, spread, own, fresh, wide, *held, sems, query_sems = scratch
    sources = (wk_ref, wv_ref, keys_ref, values_ref)
    moves = [pltpu.make_async_copy(s, t, sems.at[i]) for i, (s, t) in enumerate(zip(sources, held[1:]))]
    members, rows, cols = stream_ref.shape
    parts = [pl.ds(i * cols, cols) for i in range(members)]
    query_moves = [
        pltpu.make_async_copy(wq_ref.at[p], held[0].at[p], query_sems.at[i]) for i, p in enumerate(parts)
    ]
    for move in (*query_moves, *moves):
        move.start()
    for ref in (spread, own, fresh):
        ref[...] = jnp.zeros(ref.shape, F32)
    heads, size = out_ref.shape[1] // keys_ref.shape[2], keys_ref.shape[2]
    width = members * cols
    total = jnp.zeros((rows, 1), F32)
    for i in range(members):
        block = stream_ref[i].astype(F32)
        wide[...] = block
        few = mine_ref.shape[0]
        mine = wide[pl.ds(pl.multiple_of(place_ref[2] * few, few), few), :]
        mine_ref[:, i * cols : (i + 1) * cols] = mine.astype(BF)
        total += jnp.sum(block * block, axis=1, keepdims=True)
    scale = lax.rsqrt(total / width + EPSILON)
    for i in range(members):
        normed[:, i * cols : (i + 1) * cols] = (stream_ref[i].astype(F32) * scale).astype(BF)
    queries = jnp.zeros((rows, out_ref.shape[1]), F32)
    for move, p in zip(query_moves, parts):
        move.wait()
        queries += jnp.dot(normed[:, p], held[0][p, :], preferred_element_type=F32)

    def project(i):
        moves[i].wait()
        return jnp.dot(normed[...], held[1 + i][...], preferred_element_type=F32)

    key_new = project(0).astype(BF).astype(F32)
    value_new = project(1).astype(BF).astype(F32)
    pad = spread.shape[1] // 3
    factor = 1.0 / math.sqrt(size)
    for h in range(heads):
        query = queries[:, h * size : (h + 1) * size]
        for i, part in enumerate(split3(query)):
            spread[:, pad * i + h, :] = part.astype(F32)
        mine = jnp.sum(query * key_new, axis=1, keepdims=True) * factor
        own[:, h, :] = jnp.broadcast_to(mine, (rows, size))
        fresh[:, h, :] = value_new

    def parts_dot(parts, cached, dim):
        result = lax.dot_general(
            parts.astype(BF), cached, (((2,), (dim,)), ((0,), (0,))), preferred_element_type=F32
        )
        return result[:, :pad] + result[:, pad : 2 * pad] + result[:, 2 * pad :]

    moves[2].wait()
    scores = parts_dot(spread[...], held[3][...], 2) * factor
    window = scores.shape[2]
    allowed = lax.broadcasted_iota(jnp.int32, scores.shape, 2) >= start_ref[...]
    masked = jnp.where(allowed, scores, -jnp.inf)
    own_score = own[...]
    highest = jnp.maximum(jnp.max(masked, axis=2, keepdims=True), own_score[:, :, :1])
    weights = jnp.exp(masked - highest)
    own_weight = jnp.exp(own_score - highest)
    denominator = jnp.sum(weights, axis=2, keepdims=True) + own_weight[:, :, :1]
    probabilities = weights / denominator
    split = jnp.concatenate([part.astype(F32) for part in split3(probabilities)], axis=1)
    moves[3].wait()
    attended = parts_dot(split, held[4][...], 1) + own_weight / denominator * fresh[...]
    own[...] = attended
    for h in range(heads):
        out_ref[:, h * size : (h + 1) * size] = own[:, h, :].astype(BF)


def attend(place, group_stream, w_query, w_key, w_value, cache_keys, cache_values, lengths):
    members, rows, cols = group_stream.shape
    window, size = cache_keys.shape[1:]
    pad = 8
    large = in_hbm((w_query, w_key, w_value, cache_keys, cache_values))
    start = jnp.broadcast_to((window - lengths)[:, None, None], (rows, pad, window))
    return pl.pallas_call(
        attend_kernel,
        in_specs=[pl.BlockSpec(memory_space=pltpu.SMEM), pl.BlockSpec(memory_space=pltpu.VMEM)]
        + [pl.BlockSpec(memory_space=pl.ANY)] * 5
        + [pl.BlockSpec(memory_space=pltpu.VMEM)],
        out_specs=[pl.BlockSpec(memory_space=pltpu.VMEM)] * 2,
        out_shape=[
            jax.ShapeDtypeStruct((rows // members, members * cols), BF),
            jax.ShapeDtypeStruct((rows, w_query.shape[1]), BF),
        ],
        scratch_shapes=[
            pltpu.VMEM((rows, members * cols), BF),
            pltpu.VMEM((rows, 3 * pad, size), F32),
            pltpu.VMEM((rows, pad, size), F32),
            pltpu.VMEM((rows, pad, size), F32),
            pltpu.VMEM((rows, cols), F32),
            *(pltpu.VMEM(a.shape, a.dtype) for a in large),
            pltpu.SemaphoreType.DMA((4,)),
            pltpu.SemaphoreType.DMA((members,)),
        ],
        compiler_params=pltpu.CompilerParams(vmem_limit_bytes=24 << 20),
        cost_estimate=pl.CostEstimate(
            flops=2 * rows * members * cols * (w_query.shape[1] + 2 * size),
            bytes_accessed=2 * members * cols * (w_query.shape[1] + 2 * size),
            transcendentals=rows * pad * window,
        ),
        name="attend",
    )(
        place,
        group_stream,
        *large,
        start.astype(jnp.int32),
    )


def split3(values):
    high = values.astype(BF)
    rest = values - high.astype(F32)
    middle = rest.astype(BF)
    return high, middle, (rest - middle.astype(F32)).astype(BF)


def prepare_kernel(*refs):
    sources, out_ref, held, sems = refs[:3], refs[3], refs[4:7], refs[7]
    moves = [pltpu.make_async_copy(s, t, sems.at[i]) for i, (s, t) in enumerate(zip(sources, held))]
    for move in moves:
        move.start()
    for move in moves:
        move.wait()
    tokens_ref, ids_ref, combine_ref = held
    rows, width = tokens_ref.shape
    experts = LANES // 4
    lane = lax.broadcasted_iota(jnp.int32, (rows, LANES), 1)
    expert = lane % experts
    chosen = jnp.zeros((rows, LANES), F32)
    weight = jnp.zeros((rows, LANES), F32)
    for k in range(ids_ref.shape[1]):
        named = ids_ref[:, k : k + 1] == expert
        chosen = jnp.where(named, 1.0, chosen)
        weight = jnp.where(named, combine_ref[:, k : k + 1], weight)
    row = lax.broadcasted_iota(jnp.int32, (rows, LANES), 0)
    rank = jnp.zeros((rows, LANES), F32)
    for r in range(rows - 1):
        rank += jnp.where(row > r, chosen[r : r + 1, :], 0.0)
    rank = jnp.where(chosen > 0.0, rank, float(CAP))
    terms = [part.astype(F32) for part in split3(weight)]
    columns = rank
    for i, term in enumerate(terms):
        columns = jnp.where(lane >= (i + 1) * experts, term, columns)
    for i in range(out_ref.shape[0]):
        out_ref[i, :, :width] = tokens_ref[...]
        out_ref[i, :, width:] = columns.astype(BF)


def prepare(tokens, expert_ids, combine, members):
    rows, width = tokens.shape
    return pl.pallas_call(
        prepare_kernel,
        in_specs=[pl.BlockSpec(memory_space=pl.ANY)] * 3,
        out_specs=pl.BlockSpec(memory_space=pltpu.VMEM),
        out_shape=jax.ShapeDtypeStruct((members, rows, width + LANES), BF),
        scratch_shapes=[
            *(pltpu.VMEM(a.shape, a.dtype) for a in (tokens, expert_ids, combine)),
            pltpu.SemaphoreType.DMA((3,)),
        ],
        compiler_params=pltpu.CompilerParams(vmem_limit_bytes=4 << 20),
        cost_estimate=pl.CostEstimate(
            flops=0, bytes_accessed=2 * members * rows * width, transcendentals=0
        ),
        name="prepare",
    )(*in_hbm((tokens, expert_ids, combine)))


def per_device(
    tokens,
    expert_ids,
    combine,
    w_gate,
    w_up,
    w_down,
    w_query,
    w_key,
    w_value,
    cache_keys,
    cache_values,
    lengths,
):
    rows_n, width = tokens.shape
    x, y, c, z = (lax.axis_index(a) for a in ("x", "y", "c", "z"))
    chips = lax.axis_size("x") * lax.axis_size("y")
    experts = 2 * chips
    members = lax.axis_size("z")
    group = rows_n * members
    hidden = w_gate.shape[2]
    cols = width // members

    sent = prepare(tokens, expert_ids, combine, members)
    own = [w_gate[0].T, w_up[0].T]
    arrived, down, *other = lax.optimization_barrier(
        (lax.all_to_all(sent, "z", 0, 0, tiled=True), w_down[0], *(shift(w, "c", 1) for w in own))
    )
    weights = own + other
    down_own = lax.all_to_all(down, "z", 1, 0, tiled=True).reshape(members, hidden, cols)
    arrived = arrived.reshape(group, width + LANES)
    group_tokens, meta = arrived[:, :width], arrived[:, width:]
    widened = group_tokens.astype(F32)
    normed = (
        widened * lax.rsqrt(jnp.mean(widened * widened, axis=-1, keepdims=True) + EPSILON)
    ).astype(BF)
    dense = jnp.concatenate([normed, meta], axis=1)

    lane = jnp.arange(LANES, dtype=jnp.int32)[None, :]
    e_own = (x * 4 + y) * 2 + c
    e_other = (x * 4 + y) * 2 + 1 - c
    masks = jnp.concatenate([lane == e_own, lane == e_other] + [lane < 0] * 6, axis=0).astype(F32)
    masks = masks.astype(BF)
    half = group // 2

    def pairs(block, axis, mask):
        return lax.ppermute(block, axis, [(i, i ^ mask) for i in range(4)])

    def near_rows(block, axis):
        return jnp.concatenate([block, pairs(block, axis, 1)], axis=0)

    sides = lambda part, axis: (shift(part, axis, 1), shift(part, axis, -1))
    a_near, b_near = near_rows(dense[:half], "x"), near_rows(dense[half:], "y")
    a_far, b_far = pairs(a_near, "x", 3), pairs(b_near, "y", 3)
    a_near_sides, b_near_sides = sides(a_near, "y"), sides(b_near, "x")
    a_far_sides, b_far_sides = sides(a_far, "y"), sides(b_far, "x")
    near = (a_near, a_far, b_near, b_far, *a_near_sides, *b_near_sides)
    far = (*a_far_sides, *b_far_sides)
    slots = expert_slots(near, masks, weights)
    slots, *far = lax.optimization_barrier((slots, *far))
    opposite = (
        shift(a_near_sides[1], "y", -1),
        shift(far[0], "y", 1),
        shift(b_near_sides[1], "x", -1),
        shift(far[2], "x", 1),
    )
    more, down_own = lax.optimization_barrier((expert_slots(far, masks, weights), down_own))
    down_other = shift(down_own, "c", 1)
    slots = jnp.concatenate([slots, more, expert_slots(opposite, masks, weights)], axis=0)
    active = ring(slots, "z")
    place = jnp.stack([x, y, z]).astype(jnp.int32)
    result = lower(place, active, down_own, down_other, chips)
    per_chip = result.shape[2]
    result = result.reshape(chips, 2 * per_chip, cols)
    returned = lax.all_to_all(result, ("x", "y"), 0, 0, tiled=True)

    rank = meta[:, :experts].astype(F32)
    weight = sum(meta[:, i * experts : (i + 1) * experts].astype(F32) for i in (1, 2, 3))
    by_core = lambda v: v.reshape(group, chips, 2)
    order = lambda v: jnp.where(c == 0, by_core(v), by_core(v)[:, :, ::-1])
    rank, weight = order(rank), order(weight)
    slot = jnp.arange(per_chip, dtype=jnp.int32)
    mine = (slot // CAP)[None, :] == (jnp.arange(group) // rows_n)[:, None]
    hit = mine[:, None, None, :] & (
        rank[..., None] == (slot % CAP).astype(F32)[None, None, None, :]
    )
    spread = jnp.where(hit, weight[..., None], 0.0).reshape(group, chips * 2 * per_chip)
    mixture = jnp.dot(
        spread,
        returned.reshape(chips * 2 * per_chip, cols).astype(F32),
        precision=lax.Precision.HIGHEST,
        preferred_element_type=F32,
    )
    block_tokens = lax.dynamic_slice(group_tokens, (jnp.int32(0), z * cols), (group, cols))
    stream_block = (block_tokens.astype(F32) + mixture).astype(BF)
    guard_args = (w_query, w_key, w_value, cache_keys[:, 0], cache_values[:, 0])
    group_stream = copies(stream_block, "z")
    stream, guard = attend(place, group_stream, *guard_args, lengths)
    return (stream, guard)


def solution(mesh):
    torus = Mesh(mesh.devices.reshape(4, 4, 2, mesh.devices.shape[1]), ("x", "y", "c", "z"))
    ep = ("x", "y", "c")
    every = (*ep, "z")
    return jax.shard_map(
        per_device,
        mesh=torus,
        in_specs=(
            P(every, None),
            P(every, None),
            P(every, None),
            P(ep, None, "z"),
            P(ep, None, "z"),
            P(ep, "z", None),
            P(None, "z"),
            P(None, "z"),
            P(None, "z"),
            P(ep, "z", None, None),
            P(ep, "z", None, None),
            P(ep),
        ),
        out_specs=(P(every, None), P(ep, "z")),
        check_vma=False,
    )
```

```python
import functools
import math

import jax
import jax.numpy as jnp
from jax import lax
from jax.experimental import pallas as pl
from jax.experimental.pallas import tpu as pltpu
from jax.sharding import Mesh
from jax.sharding import PartitionSpec as P

EPSILON = 1e-06
BF = jnp.bfloat16
F32 = jnp.float32
LANES = 128
CAP = 3


def shift(values, axis, step):
    size = lax.axis_size(axis)
    return lax.ppermute(values, axis, [(i, (i - step) % size) for i in range(size)])


def ring(block, axis):
    size = lax.axis_size(axis)
    pieces = [block] + [None] * (size - 1)
    after = before = block
    for d in range(1, size // 2):
        after, before = shift(after, axis, 1), shift(before, axis, -1)
        pieces[d], pieces[size - d] = after, before
    mid = block.shape[0] // 2
    farthest = shift(after[:mid], axis, 1), shift(before[mid:], axis, -1)
    pieces[size // 2] = jnp.concatenate(farthest, axis=0)
    return pieces


def copies(values, axis):
    size = lax.axis_size(axis)
    return lax.all_to_all(
        jnp.broadcast_to(values[None], (size, *values.shape)), axis, 0, 0, tiled=True
    )


def in_hbm(arrays):
    return [pltpu.with_memory_space_constraint(a, pltpu.HBM) for a in arrays]


def expert_kernel(sizes, steps, mask_ref, *refs):
    n = len(sizes)
    rows, meta = refs[:n], refs[n : 2 * n]
    w_refs = refs[2 * n : 2 * n + 4]
    out_ref, joined, totals = refs[2 * n + 4 :]
    k = pl.program_id(0)
    hidden = w_refs[0].shape[0]
    at = 0
    for m, row_ref in zip(sizes, rows):
        joined[at : at + m, :] = row_ref[...]
        at += m
    part = lax.dot_general(
        joined[...],
        jnp.concatenate([w_ref[...] for w_ref in w_refs], axis=0),
        (((1,), (1,)), ((), ())),
        preferred_element_type=F32,
    )

    @pl.when(k == 0)
    def _():
        totals[...] = part

    @pl.when(k > 0)
    def _():
        totals[...] += part

    @pl.when(k == steps - 1)
    def _():
        slots = out_ref.shape[0]
        held = lax.dot_general(
            mask_ref[...],
            jnp.concatenate([m_ref[...] for m_ref in meta], axis=0),
            (((1,), (1,)), ((), ())),
            preferred_element_type=F32,
        )
        s = lax.broadcasted_iota(jnp.int32, (slots, 1), 0)
        same = lax.broadcasted_iota(jnp.int32, (slots, at), 1) // 8 == s // CAP
        rank = (s % CAP).astype(F32)
        for j in range(2):
            base = 2 * j * hidden
            gate = totals[:, base : base + hidden]
            up = totals[:, base + hidden : base + 2 * hidden]
            active = (gate / (1.0 + jnp.exp(-gate)) * up).astype(BF)
            pick = jnp.where(same & (held[j : j + 1, :] == rank), 1.0, 0.0).astype(BF)
            packed = jnp.dot(pick, active, preferred_element_type=F32)
            out_ref[:, j * hidden : (j + 1) * hidden] = packed.astype(BF)


def expert_slots(pieces, masks, weights, on_chip=False):
    hidden, depth = weights[0].shape
    chunk = 1024
    steps = depth // chunk
    sizes = tuple(p.shape[0] for p in pieces)
    in_specs = [pl.BlockSpec((8, LANES), lambda k: (0, 0))]
    in_specs += [pl.BlockSpec((m, chunk), lambda k: (0, k)) for m in sizes]
    in_specs += [pl.BlockSpec((m, LANES), lambda k: (0, depth // LANES)) for m in sizes]
    in_specs += [pl.BlockSpec((hidden, chunk), lambda k: (0, k))] * 4
    pieces, weights = pieces if on_chip else in_hbm(pieces), in_hbm(weights)
    total = sum(sizes)
    slots = total // 8 * CAP
    return pl.pallas_call(
        functools.partial(expert_kernel, sizes, steps),
        grid=(steps,),
        in_specs=in_specs,
        out_specs=pl.BlockSpec((slots, 2 * hidden), lambda k: (0, 0)),
        out_shape=jax.ShapeDtypeStruct((slots, 2 * hidden), BF),
        scratch_shapes=[
            pltpu.VMEM((total, chunk), BF),
            pltpu.VMEM((total, 4 * hidden), F32),
        ],
        compiler_params=pltpu.CompilerParams(vmem_limit_bytes=20 << 20),
        cost_estimate=pl.CostEstimate(
            flops=8 * total * depth * hidden,
            bytes_accessed=8 * depth * hidden + 2 * total * depth,
            transcendentals=2 * total * hidden,
        ),
        name="expert_slots",
    )(masks, *pieces, *pieces, *weights)


PIECES = (
    *((h, 0, i) for h in (0, 1) for i in (0, 2)),
    *((h, o, 0) for h in (0, 1) for o in (1, 3)),
    *((h, o, 2) for h in (0, 1) for o in (1, 3)),
    *((h, 2, i) for i in (0, 2) for h in (0, 1)),
)


def lower_kernel(place_ref, own_ref, other_ref, *refs):
    members, hidden, _ = own_ref.shape
    active_refs, refs = refs[:members], refs[members:]
    out_ref, first_sum, second_sum, placed, own_held, other_held, sems = refs
    sums = (first_sum, second_sum)
    pairs = ((own_ref, own_held), (other_ref, other_held))
    z = place_ref[2]
    moves = []
    for d in range(members):
        at = (z + d) % members
        moves.append(
            [pltpu.make_async_copy(s.at[at], t.at[d], sems.at[i, d]) for i, (s, t) in enumerate(pairs)]
        )
        for move in moves[d]:
            move.start()
    for d in range(members):
        for j, held in enumerate((own_held, other_held)):
            moves[d][j].wait()
            span = slice(j * hidden, (j + 1) * hidden)
            part = jnp.dot(active_refs[d][:, span], held[d], preferred_element_type=F32)
            if d == 0:
                sums[j][...] = part
            else:
                sums[j][...] += part
    x, y = place_ref[0], place_ref[1]
    per = placed.shape[2] // 2
    for p, (h, outer, inner) in enumerate(PIECES):
        for i in range(2):
            at = (2 * p + i) * per
            step = (0, 1, 3, 2)[inner + i]
            if h == 0:
                chip = (x ^ step) * 4 + (y + outer) % 4
            else:
                chip = (x + outer) % 4 * 4 + (y ^ step)
            for j in range(2):
                placed[chip, j, h * per : (h + 1) * per, :] = sums[j][at : at + per, :]
    out_ref[...] = placed[...].astype(BF)


def lower(place, active, down_own, down_other, chips):
    members, hidden, cols = down_own.shape
    down_own, down_other = in_hbm((down_own, down_other))
    slots = active[0].shape[0]
    per_chip = slots // chips
    return pl.pallas_call(
        lower_kernel,
        in_specs=[pl.BlockSpec(memory_space=pltpu.SMEM)]
        + [pl.BlockSpec(memory_space=pl.ANY)] * 2
        + [pl.BlockSpec(memory_space=pltpu.VMEM)] * members,
        out_specs=pl.BlockSpec(memory_space=pltpu.VMEM),
        out_shape=jax.ShapeDtypeStruct((chips, 2, per_chip, cols), BF),
        scratch_shapes=[
            pltpu.VMEM((slots, cols), F32),
            pltpu.VMEM((slots, cols), F32),
            pltpu.VMEM((chips, 2, per_chip, cols), F32),
            pltpu.VMEM(down_own.shape, BF),
            pltpu.VMEM(down_other.shape, BF),
            pltpu.SemaphoreType.DMA((2, members)),
        ],
        compiler_params=pltpu.CompilerParams(vmem_limit_bytes=24 << 20),
        cost_estimate=pl.CostEstimate(
            flops=4 * members * slots * hidden * cols,
            bytes_accessed=4 * members * hidden * (slots + cols),
            transcendentals=0,
        ),
        name="lower",
    )(place, down_own, down_other, *active)


def attend_kernel(
    place_ref, stream_ref, wq_ref, wk_ref, wv_ref, keys_ref, values_ref, start_ref, mine_ref, out_ref, *scratch
):
    normed, spread, own, fresh, wide, *held, sems, query_sems = scratch
    sources = (wk_ref, wv_ref, keys_ref, values_ref)
    moves = [pltpu.make_async_copy(s, t, sems.at[i]) for i, (s, t) in enumerate(zip(sources, held[1:]))]
    members, rows, cols = stream_ref.shape
    parts = [pl.ds(i * cols, cols) for i in range(members)]
    query_moves = [
        pltpu.make_async_copy(wq_ref.at[p], held[0].at[p], query_sems.at[i]) for i, p in enumerate(parts)
    ]
    for move in (*query_moves, *moves):
        move.start()
    for ref in (spread, own, fresh):
        ref[...] = jnp.zeros(ref.shape, F32)
    heads, size = out_ref.shape[1] // keys_ref.shape[2], keys_ref.shape[2]
    width = members * cols
    total = jnp.zeros((rows, 1), F32)
    for i in range(members):
        block = stream_ref[i].astype(F32)
        wide[...] = block
        few = mine_ref.shape[0]
        mine = wide[pl.ds(pl.multiple_of(place_ref[2] * few, few), few), :]
        mine_ref[:, i * cols : (i + 1) * cols] = mine.astype(BF)
        total += jnp.sum(block * block, axis=1, keepdims=True)
    scale = lax.rsqrt(total / width + EPSILON)
    for i in range(members):
        normed[:, i * cols : (i + 1) * cols] = (stream_ref[i].astype(F32) * scale).astype(BF)
    queries = jnp.zeros((rows, out_ref.shape[1]), F32)
    for move, p in zip(query_moves, parts):
        move.wait()
        queries += jnp.dot(normed[:, p], held[0][p, :], preferred_element_type=F32)

    def project(i):
        moves[i].wait()
        return jnp.dot(normed[...], held[1 + i][...], preferred_element_type=F32)

    key_new = project(0).astype(BF).astype(F32)
    value_new = project(1).astype(BF).astype(F32)
    pad = spread.shape[1] // 3
    factor = 1.0 / math.sqrt(size)
    for h in range(heads):
        query = queries[:, h * size : (h + 1) * size]
        for i, part in enumerate(split3(query)):
            spread[:, pad * i + h, :] = part.astype(F32)
        mine = jnp.sum(query * key_new, axis=1, keepdims=True) * factor
        own[:, h, :] = jnp.broadcast_to(mine, (rows, size))
        fresh[:, h, :] = value_new

    def parts_dot(parts, cached, dim):
        result = lax.dot_general(
            parts.astype(BF), cached, (((2,), (dim,)), ((0,), (0,))), preferred_element_type=F32
        )
        return result[:, :pad] + result[:, pad : 2 * pad] + result[:, 2 * pad :]

    moves[2].wait()
    scores = parts_dot(spread[...], held[3][...], 2) * factor
    window = scores.shape[2]
    allowed = lax.broadcasted_iota(jnp.int32, scores.shape, 2) >= start_ref[...]
    masked = jnp.where(allowed, scores, -jnp.inf)
    own_score = own[...]
    highest = jnp.maximum(jnp.max(masked, axis=2, keepdims=True), own_score[:, :, :1])
    weights = jnp.exp(masked - highest)
    own_weight = jnp.exp(own_score - highest)
    denominator = jnp.sum(weights, axis=2, keepdims=True) + own_weight[:, :, :1]
    probabilities = weights / denominator
    split = jnp.concatenate([part.astype(F32) for part in split3(probabilities)], axis=1)
    moves[3].wait()
    attended = parts_dot(split, held[4][...], 1) + own_weight / denominator * fresh[...]
    own[...] = attended
    for h in range(heads):
        out_ref[:, h * size : (h + 1) * size] = own[:, h, :].astype(BF)


def attend(place, group_stream, w_query, w_key, w_value, cache_keys, cache_values, lengths):
    members, rows, cols = group_stream.shape
    window, size = cache_keys.shape[1:]
    pad = 8
    large = in_hbm((w_query, w_key, w_value, cache_keys, cache_values))
    start = jnp.broadcast_to((window - lengths)[:, None, None], (rows, pad, window))
    return pl.pallas_call(
        attend_kernel,
        in_specs=[pl.BlockSpec(memory_space=pltpu.SMEM), pl.BlockSpec(memory_space=pltpu.VMEM)]
        + [pl.BlockSpec(memory_space=pl.ANY)] * 5
        + [pl.BlockSpec(memory_space=pltpu.VMEM)],
        out_specs=[pl.BlockSpec(memory_space=pltpu.VMEM)] * 2,
        out_shape=[
            jax.ShapeDtypeStruct((rows // members, members * cols), BF),
            jax.ShapeDtypeStruct((rows, w_query.shape[1]), BF),
        ],
        scratch_shapes=[
            pltpu.VMEM((rows, members * cols), BF),
            pltpu.VMEM((rows, 3 * pad, size), F32),
            pltpu.VMEM((rows, pad, size), F32),
            pltpu.VMEM((rows, pad, size), F32),
            pltpu.VMEM((rows, cols), F32),
            *(pltpu.VMEM(a.shape, a.dtype) for a in large),
            pltpu.SemaphoreType.DMA((4,)),
            pltpu.SemaphoreType.DMA((members,)),
        ],
        compiler_params=pltpu.CompilerParams(vmem_limit_bytes=24 << 20),
        cost_estimate=pl.CostEstimate(
            flops=2 * rows * members * cols * (w_query.shape[1] + 2 * size),
            bytes_accessed=2 * members * cols * (w_query.shape[1] + 2 * size),
            transcendentals=rows * pad * window,
        ),
        name="attend",
    )(
        place,
        group_stream,
        *large,
        start.astype(jnp.int32),
    )


def split3(values):
    high = values.astype(BF)
    rest = values - high.astype(F32)
    middle = rest.astype(BF)
    return high, middle, (rest - middle.astype(F32)).astype(BF)


def prepare_kernel(*refs):
    sources, out_ref, held, sems = refs[:3], refs[3], refs[4:7], refs[7]
    moves = [pltpu.make_async_copy(s, t, sems.at[i]) for i, (s, t) in enumerate(zip(sources, held))]
    for move in moves:
        move.start()
    for move in moves:
        move.wait()
    tokens_ref, ids_ref, combine_ref = held
    rows, width = tokens_ref.shape
    experts = LANES // 4
    lane = lax.broadcasted_iota(jnp.int32, (rows, LANES), 1)
    expert = lane % experts
    chosen = jnp.zeros((rows, LANES), F32)
    weight = jnp.zeros((rows, LANES), F32)
    for k in range(ids_ref.shape[1]):
        named = ids_ref[:, k : k + 1] == expert
        chosen = jnp.where(named, 1.0, chosen)
        weight = jnp.where(named, combine_ref[:, k : k + 1], weight)
    row = lax.broadcasted_iota(jnp.int32, (rows, LANES), 0)
    rank = jnp.zeros((rows, LANES), F32)
    for r in range(rows - 1):
        rank += jnp.where(row > r, chosen[r : r + 1, :], 0.0)
    rank = jnp.where(chosen > 0.0, rank, float(CAP))
    terms = [part.astype(F32) for part in split3(weight)]
    columns = rank
    for i, term in enumerate(terms):
        columns = jnp.where(lane >= (i + 1) * experts, term, columns)
    for i in range(out_ref.shape[0]):
        out_ref[i, :, :width] = tokens_ref[...]
        out_ref[i, :, width:] = columns.astype(BF)


def prepare(tokens, expert_ids, combine, members):
    rows, width = tokens.shape
    return pl.pallas_call(
        prepare_kernel,
        in_specs=[pl.BlockSpec(memory_space=pl.ANY)] * 3,
        out_specs=pl.BlockSpec(memory_space=pltpu.VMEM),
        out_shape=jax.ShapeDtypeStruct((members, rows, width + LANES), BF),
        scratch_shapes=[
            *(pltpu.VMEM(a.shape, a.dtype) for a in (tokens, expert_ids, combine)),
            pltpu.SemaphoreType.DMA((3,)),
        ],
        compiler_params=pltpu.CompilerParams(vmem_limit_bytes=4 << 20),
        cost_estimate=pl.CostEstimate(
            flops=0, bytes_accessed=2 * members * rows * width, transcendentals=0
        ),
        name="prepare",
    )(*in_hbm((tokens, expert_ids, combine)))


def per_device(
    tokens,
    expert_ids,
    combine,
    w_gate,
    w_up,
    w_down,
    w_query,
    w_key,
    w_value,
    cache_keys,
    cache_values,
    lengths,
):
    rows_n, width = tokens.shape
    x, y, c, z = (lax.axis_index(a) for a in ("x", "y", "c", "z"))
    chips = lax.axis_size("x") * lax.axis_size("y")
    experts = 2 * chips
    members = lax.axis_size("z")
    group = rows_n * members
    hidden = w_gate.shape[2]
    cols = width // members

    sent = prepare(tokens, expert_ids, combine, members)
    own = [w_gate[0].T, w_up[0].T]
    arrived, down, *other = lax.optimization_barrier(
        (lax.all_to_all(sent, "z", 0, 0, tiled=True), w_down[0], *(shift(w, "c", 1) for w in own))
    )
    weights = own + other
    down_own = lax.all_to_all(down, "z", 1, 0, tiled=True).reshape(members, hidden, cols)
    arrived = arrived.reshape(group, width + LANES)
    group_tokens, meta = arrived[:, :width], arrived[:, width:]
    widened = group_tokens.astype(F32)
    normed = (
        widened * lax.rsqrt(jnp.mean(widened * widened, axis=-1, keepdims=True) + EPSILON)
    ).astype(BF)
    dense = jnp.concatenate([normed, meta], axis=1)

    lane = jnp.arange(LANES, dtype=jnp.int32)[None, :]
    e_own = (x * 4 + y) * 2 + c
    e_other = (x * 4 + y) * 2 + 1 - c
    masks = jnp.concatenate([lane == e_own, lane == e_other] + [lane < 0] * 6, axis=0).astype(F32)
    masks = masks.astype(BF)
    half = group // 2

    def pairs(block, axis, mask):
        return lax.ppermute(block, axis, [(i, i ^ mask) for i in range(4)])

    def near_rows(block, axis):
        return jnp.concatenate([block, pairs(block, axis, 1)], axis=0)

    sides = lambda part, axis: (shift(part, axis, 1), shift(part, axis, -1))
    a_near, b_near = near_rows(dense[:half], "x"), near_rows(dense[half:], "y")
    a_far, b_far = pairs(a_near, "x", 3), pairs(b_near, "y", 3)
    a_near_sides, b_near_sides = sides(a_near, "y"), sides(b_near, "x")
    a_far_sides, b_far_sides = sides(a_far, "y"), sides(b_far, "x")
    near = (a_near, a_far, b_near, b_far, *a_near_sides, *b_near_sides)
    far = (*a_far_sides, *b_far_sides)
    slots = expert_slots(near, masks, weights)
    slots, *far = lax.optimization_barrier((slots, *far))
    far += [shift(a_near_sides[1], "y", -1), shift(b_near_sides[1], "x", -1)]
    opposite = (shift(far[0], "y", 1), shift(far[2], "x", 1))
    more, down_own = lax.optimization_barrier((expert_slots(far, masks, weights), down_own))
    down_other = shift(down_own, "c", 1)
    slots = jnp.concatenate([slots, more, expert_slots(opposite, masks, weights, on_chip=True)], axis=0)
    active = ring(slots, "z")
    place = jnp.stack([x, y, z]).astype(jnp.int32)
    result = lower(place, active, down_own, down_other, chips)
    per_chip = result.shape[2]
    result = result.reshape(chips, 2 * per_chip, cols)
    returned = lax.all_to_all(result, ("x", "y"), 0, 0, tiled=True)

    rank = meta[:, :experts].astype(F32)
    weight = sum(meta[:, i * experts : (i + 1) * experts].astype(F32) for i in (1, 2, 3))
    by_core = lambda v: v.reshape(group, chips, 2)
    order = lambda v: jnp.where(c == 0, by_core(v), by_core(v)[:, :, ::-1])
    rank, weight = order(rank), order(weight)
    slot = jnp.arange(per_chip, dtype=jnp.int32)
    mine = (slot // CAP)[None, :] == (jnp.arange(group) // rows_n)[:, None]
    hit = mine[:, None, None, :] & (
        rank[..., None] == (slot % CAP).astype(F32)[None, None, None, :]
    )
    spread = jnp.where(hit, weight[..., None], 0.0).reshape(group, chips * 2 * per_chip)
    mixture = jnp.dot(
        spread,
        returned.reshape(chips * 2 * per_chip, cols).astype(F32),
        precision=lax.Precision.HIGHEST,
        preferred_element_type=F32,
    )
    block_tokens = lax.dynamic_slice(group_tokens, (jnp.int32(0), z * cols), (group, cols))
    stream_block = (block_tokens.astype(F32) + mixture).astype(BF)
    guard_args = (w_query, w_key, w_value, cache_keys[:, 0], cache_values[:, 0])
    group_stream = copies(stream_block, "z")
    stream, guard = attend(place, group_stream, *guard_args, lengths)
    return (stream, guard)


def solution(mesh):
    torus = Mesh(mesh.devices.reshape(4, 4, 2, mesh.devices.shape[1]), ("x", "y", "c", "z"))
    ep = ("x", "y", "c")
    every = (*ep, "z")
    return jax.shard_map(
        per_device,
        mesh=torus,
        in_specs=(
            P(every, None),
            P(every, None),
            P(every, None),
            P(ep, None, "z"),
            P(ep, None, "z"),
            P(ep, "z", None),
            P(None, "z"),
            P(None, "z"),
            P(None, "z"),
            P(ep, "z", None, None),
            P(ep, "z", None, None),
            P(ep),
        ),
        out_specs=(P(every, None), P(ep, "z")),
        check_vma=False,
    )
```

```python
import functools
import math

import jax
import jax.numpy as jnp
from jax import lax
from jax.experimental import pallas as pl
from jax.experimental.pallas import tpu as pltpu
from jax.sharding import Mesh
from jax.sharding import PartitionSpec as P

EPSILON = 1e-06
BF = jnp.bfloat16
F32 = jnp.float32
LANES = 128
CAP = 3


def shift(values, axis, step):
    size = lax.axis_size(axis)
    return lax.ppermute(values, axis, [(i, (i - step) % size) for i in range(size)])


def ring(block, axis):
    size = lax.axis_size(axis)
    pieces = [block] + [None] * (size - 1)
    after = before = block
    for d in range(1, size // 2):
        after, before = shift(after, axis, 1), shift(before, axis, -1)
        pieces[d], pieces[size - d] = after, before
    mid = block.shape[0] // 2
    farthest = shift(after[:mid], axis, 1), shift(before[mid:], axis, -1)
    pieces[size // 2] = jnp.concatenate(farthest, axis=0)
    return pieces


def copies(values, axis):
    size = lax.axis_size(axis)
    return lax.all_to_all(
        jnp.broadcast_to(values[None], (size, *values.shape)), axis, 0, 0, tiled=True
    )


def in_hbm(arrays):
    return [pltpu.with_memory_space_constraint(a, pltpu.HBM) for a in arrays]


def expert_kernel(sizes, steps, mask_ref, *refs):
    n = len(sizes)
    rows, meta = refs[:n], refs[n : 2 * n]
    w_refs = refs[2 * n : 2 * n + 4]
    out_ref, joined, totals = refs[2 * n + 4 :]
    k = pl.program_id(0)
    hidden = w_refs[0].shape[0]
    at = 0
    for m, row_ref in zip(sizes, rows):
        joined[at : at + m, :] = row_ref[...]
        at += m
    part = lax.dot_general(
        joined[...],
        jnp.concatenate([w_ref[...] for w_ref in w_refs], axis=0),
        (((1,), (1,)), ((), ())),
        preferred_element_type=F32,
    )

    @pl.when(k == 0)
    def _():
        totals[...] = part

    @pl.when(k > 0)
    def _():
        totals[...] += part

    @pl.when(k == steps - 1)
    def _():
        slots = out_ref.shape[0]
        held = lax.dot_general(
            mask_ref[...],
            jnp.concatenate([m_ref[...] for m_ref in meta], axis=0),
            (((1,), (1,)), ((), ())),
            preferred_element_type=F32,
        )
        s = lax.broadcasted_iota(jnp.int32, (slots, 1), 0)
        same = lax.broadcasted_iota(jnp.int32, (slots, at), 1) // 8 == s // CAP
        rank = (s % CAP).astype(F32)
        for j in range(2):
            base = 2 * j * hidden
            gate = totals[:, base : base + hidden]
            up = totals[:, base + hidden : base + 2 * hidden]
            active = (gate / (1.0 + jnp.exp(-gate)) * up).astype(BF)
            pick = jnp.where(same & (held[j : j + 1, :] == rank), 1.0, 0.0).astype(BF)
            packed = jnp.dot(pick, active, preferred_element_type=F32)
            out_ref[:, j * hidden : (j + 1) * hidden] = packed.astype(BF)


def expert_slots(pieces, masks, weights, on_chip=False):
    hidden, depth = weights[0].shape
    chunk = 2048
    steps = depth // chunk
    sizes = tuple(p.shape[0] for p in pieces)
    in_specs = [pl.BlockSpec((8, LANES), lambda k: (0, 0))]
    in_specs += [pl.BlockSpec((m, chunk), lambda k: (0, k)) for m in sizes]
    in_specs += [pl.BlockSpec((m, LANES), lambda k: (0, depth // LANES)) for m in sizes]
    in_specs += [pl.BlockSpec((hidden, chunk), lambda k: (0, k))] * 4
    pieces, weights = pieces if on_chip else in_hbm(pieces), in_hbm(weights)
    total = sum(sizes)
    slots = total // 8 * CAP
    return pl.pallas_call(
        functools.partial(expert_kernel, sizes, steps),
        grid=(steps,),
        in_specs=in_specs,
        out_specs=pl.BlockSpec((slots, 2 * hidden), lambda k: (0, 0)),
        out_shape=jax.ShapeDtypeStruct((slots, 2 * hidden), BF),
        scratch_shapes=[
            pltpu.VMEM((total, chunk), BF),
            pltpu.VMEM((total, 4 * hidden), F32),
        ],
        compiler_params=pltpu.CompilerParams(vmem_limit_bytes=28 << 20),
        cost_estimate=pl.CostEstimate(
            flops=8 * total * depth * hidden,
            bytes_accessed=8 * depth * hidden + 2 * total * depth,
            transcendentals=2 * total * hidden,
        ),
        name="expert_slots",
    )(masks, *pieces, *pieces, *weights)


PIECES = (
    *((h, 0, i) for h in (0, 1) for i in (0, 2)),
    *((h, o, 0) for h in (0, 1) for o in (1, 3)),
    *((h, o, 2) for h in (0, 1) for o in (1, 3)),
    *((h, 2, i) for h in (0, 1) for i in (0, 2)),
)


def lower_kernel(place_ref, own_ref, other_ref, *refs):
    members, hidden, _ = own_ref.shape
    active_refs, refs = refs[:members], refs[members:]
    out_ref, first_sum, second_sum, placed, own_held, other_held, sems = refs
    sums = (first_sum, second_sum)
    pairs = ((own_ref, own_held), (other_ref, other_held))
    z = place_ref[2]
    moves = []
    for d in range(members):
        at = (z + d) % members
        moves.append(
            [pltpu.make_async_copy(s.at[at], t.at[d], sems.at[i, d]) for i, (s, t) in enumerate(pairs)]
        )
        for move in moves[d]:
            move.start()
    for d in range(members):
        for j, held in enumerate((own_held, other_held)):
            moves[d][j].wait()
            span = slice(j * hidden, (j + 1) * hidden)
            part = jnp.dot(active_refs[d][:, span], held[d], preferred_element_type=F32)
            if d == 0:
                sums[j][...] = part
            else:
                sums[j][...] += part
    x, y = place_ref[0], place_ref[1]
    per = placed.shape[2] // 2
    for p, (h, outer, inner) in enumerate(PIECES):
        for i in range(2):
            at = (2 * p + i) * per
            step = (0, 1, 3, 2)[inner + i]
            if h == 0:
                chip = (x ^ step) * 4 + (y + outer) % 4
            else:
                chip = (x + outer) % 4 * 4 + (y ^ step)
            for j in range(2):
                placed[chip, j, h * per : (h + 1) * per, :] = sums[j][at : at + per, :]
    out_ref[...] = placed[...].astype(BF)


def lower(place, active, down_own, down_other, chips):
    members, hidden, cols = down_own.shape
    down_own, down_other = in_hbm((down_own, down_other))
    slots = active[0].shape[0]
    per_chip = slots // chips
    return pl.pallas_call(
        lower_kernel,
        in_specs=[pl.BlockSpec(memory_space=pltpu.SMEM)]
        + [pl.BlockSpec(memory_space=pl.ANY)] * 2
        + [pl.BlockSpec(memory_space=pltpu.VMEM)] * members,
        out_specs=pl.BlockSpec(memory_space=pltpu.VMEM),
        out_shape=jax.ShapeDtypeStruct((chips, 2, per_chip, cols), BF),
        scratch_shapes=[
            pltpu.VMEM((slots, cols), F32),
            pltpu.VMEM((slots, cols), F32),
            pltpu.VMEM((chips, 2, per_chip, cols), F32),
            pltpu.VMEM(down_own.shape, BF),
            pltpu.VMEM(down_other.shape, BF),
            pltpu.SemaphoreType.DMA((2, members)),
        ],
        compiler_params=pltpu.CompilerParams(vmem_limit_bytes=24 << 20),
        cost_estimate=pl.CostEstimate(
            flops=4 * members * slots * hidden * cols,
            bytes_accessed=4 * members * hidden * (slots + cols),
            transcendentals=0,
        ),
        name="lower",
    )(place, down_own, down_other, *active)


def attend_kernel(
    place_ref, stream_ref, wq_ref, wk_ref, wv_ref, keys_ref, values_ref, start_ref, mine_ref, out_ref, *scratch
):
    normed, spread, own, fresh, wide, *held, sems, query_sems = scratch
    sources = (wk_ref, wv_ref, keys_ref, values_ref)
    moves = [pltpu.make_async_copy(s, t, sems.at[i]) for i, (s, t) in enumerate(zip(sources, held[1:]))]
    members, rows, cols = stream_ref.shape
    parts = [pl.ds(i * cols, cols) for i in range(members)]
    query_moves = [
        pltpu.make_async_copy(wq_ref.at[p], held[0].at[p], query_sems.at[i]) for i, p in enumerate(parts)
    ]
    for move in (*query_moves, *moves):
        move.start()
    for ref in (spread, own, fresh):
        ref[...] = jnp.zeros(ref.shape, F32)
    heads, size = out_ref.shape[1] // keys_ref.shape[2], keys_ref.shape[2]
    width = members * cols
    total = jnp.zeros((rows, 1), F32)
    for i in range(members):
        block = stream_ref[i].astype(F32)
        wide[...] = block
        few = mine_ref.shape[0]
        mine = wide[pl.ds(pl.multiple_of(place_ref[2] * few, few), few), :]
        mine_ref[:, i * cols : (i + 1) * cols] = mine.astype(BF)
        total += jnp.sum(block * block, axis=1, keepdims=True)
    scale = lax.rsqrt(total / width + EPSILON)
    for i in range(members):
        normed[:, i * cols : (i + 1) * cols] = (stream_ref[i].astype(F32) * scale).astype(BF)
    queries = jnp.zeros((rows, out_ref.shape[1]), F32)
    for move, p in zip(query_moves, parts):
        move.wait()
        queries += jnp.dot(normed[:, p], held[0][p, :], preferred_element_type=F32)

    def project(i):
        moves[i].wait()
        return jnp.dot(normed[...], held[1 + i][...], preferred_element_type=F32)

    key_new = project(0).astype(BF).astype(F32)
    value_new = project(1).astype(BF).astype(F32)
    pad = spread.shape[1] // 3
    factor = 1.0 / math.sqrt(size)
    for h in range(heads):
        query = queries[:, h * size : (h + 1) * size]
        for i, part in enumerate(split3(query)):
            spread[:, pad * i + h, :] = part.astype(F32)
        mine = jnp.sum(query * key_new, axis=1, keepdims=True) * factor
        own[:, h, :] = jnp.broadcast_to(mine, (rows, size))
        fresh[:, h, :] = value_new

    def parts_dot(parts, cached, dim):
        result = lax.dot_general(
            parts.astype(BF), cached, (((2,), (dim,)), ((0,), (0,))), preferred_element_type=F32
        )
        return result[:, :pad] + result[:, pad : 2 * pad] + result[:, 2 * pad :]

    moves[2].wait()
    scores = parts_dot(spread[...], held[3][...], 2) * factor
    window = scores.shape[2]
    allowed = lax.broadcasted_iota(jnp.int32, scores.shape, 2) >= start_ref[...]
    masked = jnp.where(allowed, scores, -jnp.inf)
    own_score = own[...]
    highest = jnp.maximum(jnp.max(masked, axis=2, keepdims=True), own_score[:, :, :1])
    weights = jnp.exp(masked - highest)
    own_weight = jnp.exp(own_score - highest)
    denominator = jnp.sum(weights, axis=2, keepdims=True) + own_weight[:, :, :1]
    probabilities = weights / denominator
    split = jnp.concatenate([part.astype(F32) for part in split3(probabilities)], axis=1)
    moves[3].wait()
    attended = parts_dot(split, held[4][...], 1) + own_weight / denominator * fresh[...]
    own[...] = attended
    for h in range(heads):
        out_ref[:, h * size : (h + 1) * size] = own[:, h, :].astype(BF)


def attend(place, group_stream, w_query, w_key, w_value, cache_keys, cache_values, lengths):
    members, rows, cols = group_stream.shape
    window, size = cache_keys.shape[1:]
    pad = 8
    large = in_hbm((w_query, w_key, w_value, cache_keys, cache_values))
    start = jnp.broadcast_to((window - lengths)[:, None, None], (rows, pad, window))
    return pl.pallas_call(
        attend_kernel,
        in_specs=[pl.BlockSpec(memory_space=pltpu.SMEM), pl.BlockSpec(memory_space=pltpu.VMEM)]
        + [pl.BlockSpec(memory_space=pl.ANY)] * 5
        + [pl.BlockSpec(memory_space=pltpu.VMEM)],
        out_specs=[pl.BlockSpec(memory_space=pltpu.VMEM)] * 2,
        out_shape=[
            jax.ShapeDtypeStruct((rows // members, members * cols), BF),
            jax.ShapeDtypeStruct((rows, w_query.shape[1]), BF),
        ],
        scratch_shapes=[
            pltpu.VMEM((rows, members * cols), BF),
            pltpu.VMEM((rows, 3 * pad, size), F32),
            pltpu.VMEM((rows, pad, size), F32),
            pltpu.VMEM((rows, pad, size), F32),
            pltpu.VMEM((rows, cols), F32),
            *(pltpu.VMEM(a.shape, a.dtype) for a in large),
            pltpu.SemaphoreType.DMA((4,)),
            pltpu.SemaphoreType.DMA((members,)),
        ],
        compiler_params=pltpu.CompilerParams(vmem_limit_bytes=24 << 20),
        cost_estimate=pl.CostEstimate(
            flops=2 * rows * members * cols * (w_query.shape[1] + 2 * size),
            bytes_accessed=2 * members * cols * (w_query.shape[1] + 2 * size),
            transcendentals=rows * pad * window,
        ),
        name="attend",
    )(
        place,
        group_stream,
        *large,
        start.astype(jnp.int32),
    )


def split3(values):
    high = values.astype(BF)
    rest = values - high.astype(F32)
    middle = rest.astype(BF)
    return high, middle, (rest - middle.astype(F32)).astype(BF)


def prepare_kernel(*refs):
    sources, out_ref, held, sems = refs[:3], refs[3], refs[4:7], refs[7]
    moves = [pltpu.make_async_copy(s, t, sems.at[i]) for i, (s, t) in enumerate(zip(sources, held))]
    for move in moves:
        move.start()
    for move in moves:
        move.wait()
    tokens_ref, ids_ref, combine_ref = held
    rows, width = tokens_ref.shape
    experts = LANES // 4
    lane = lax.broadcasted_iota(jnp.int32, (rows, LANES), 1)
    expert = lane % experts
    chosen = jnp.zeros((rows, LANES), F32)
    weight = jnp.zeros((rows, LANES), F32)
    for k in range(ids_ref.shape[1]):
        named = ids_ref[:, k : k + 1] == expert
        chosen = jnp.where(named, 1.0, chosen)
        weight = jnp.where(named, combine_ref[:, k : k + 1], weight)
    row = lax.broadcasted_iota(jnp.int32, (rows, LANES), 0)
    rank = jnp.zeros((rows, LANES), F32)
    for r in range(rows - 1):
        rank += jnp.where(row > r, chosen[r : r + 1, :], 0.0)
    rank = jnp.where(chosen > 0.0, rank, float(CAP))
    terms = [part.astype(F32) for part in split3(weight)]
    columns = rank
    for i, term in enumerate(terms):
        columns = jnp.where(lane >= (i + 1) * experts, term, columns)
    for i in range(out_ref.shape[0]):
        out_ref[i, :, :width] = tokens_ref[...]
        out_ref[i, :, width:] = columns.astype(BF)


def prepare(tokens, expert_ids, combine, members):
    rows, width = tokens.shape
    return pl.pallas_call(
        prepare_kernel,
        in_specs=[pl.BlockSpec(memory_space=pl.ANY)] * 3,
        out_specs=pl.BlockSpec(memory_space=pltpu.VMEM),
        out_shape=jax.ShapeDtypeStruct((members, rows, width + LANES), BF),
        scratch_shapes=[
            *(pltpu.VMEM(a.shape, a.dtype) for a in (tokens, expert_ids, combine)),
            pltpu.SemaphoreType.DMA((3,)),
        ],
        compiler_params=pltpu.CompilerParams(vmem_limit_bytes=4 << 20),
        cost_estimate=pl.CostEstimate(
            flops=0, bytes_accessed=2 * members * rows * width, transcendentals=0
        ),
        name="prepare",
    )(*in_hbm((tokens, expert_ids, combine)))


def per_device(
    tokens,
    expert_ids,
    combine,
    w_gate,
    w_up,
    w_down,
    w_query,
    w_key,
    w_value,
    cache_keys,
    cache_values,
    lengths,
):
    rows_n, width = tokens.shape
    x, y, c, z = (lax.axis_index(a) for a in ("x", "y", "c", "z"))
    chips = lax.axis_size("x") * lax.axis_size("y")
    experts = 2 * chips
    members = lax.axis_size("z")
    group = rows_n * members
    hidden = w_gate.shape[2]
    cols = width // members

    sent = prepare(tokens, expert_ids, combine, members)
    own = [w_gate[0].T, w_up[0].T]
    arrived, down, *other = lax.optimization_barrier(
        (lax.all_to_all(sent, "z", 0, 0, tiled=True), w_down[0], *(shift(w, "c", 1) for w in own))
    )
    weights = own + other
    down_own = lax.all_to_all(down, "z", 1, 0, tiled=True).reshape(members, hidden, cols)
    arrived = arrived.reshape(group, width + LANES)
    group_tokens, meta = arrived[:, :width], arrived[:, width:]
    widened = group_tokens.astype(F32)
    normed = (
        widened * lax.rsqrt(jnp.mean(widened * widened, axis=-1, keepdims=True) + EPSILON)
    ).astype(BF)
    dense = jnp.concatenate([normed, meta], axis=1)

    lane = jnp.arange(LANES, dtype=jnp.int32)[None, :]
    e_own = (x * 4 + y) * 2 + c
    e_other = (x * 4 + y) * 2 + 1 - c
    masks = jnp.concatenate([lane == e_own, lane == e_other] + [lane < 0] * 6, axis=0).astype(F32)
    masks = masks.astype(BF)
    half = group // 2

    def pairs(block, axis, mask):
        return lax.ppermute(block, axis, [(i, i ^ mask) for i in range(4)])

    def near_rows(block, axis):
        return jnp.concatenate([block, pairs(block, axis, 1)], axis=0)

    sides = lambda part, axis: (shift(part, axis, 1), shift(part, axis, -1))
    a_near, b_near = near_rows(dense[:half], "x"), near_rows(dense[half:], "y")
    a_far, b_far = pairs(a_near, "x", 3), pairs(b_near, "y", 3)
    a_near_sides, b_near_sides = sides(a_near, "y"), sides(b_near, "x")
    a_far_sides, b_far_sides = sides(a_far, "y"), sides(b_far, "x")
    near = (a_near, a_far, b_near, b_far, *a_near_sides, *b_near_sides)
    far = (*a_far_sides, *b_far_sides)
    slots = expert_slots(near, masks, weights)
    slots, *far = lax.optimization_barrier((slots, *far))
    opposite = (
        shift(a_near_sides[1], "y", -1),
        shift(far[0], "y", 1),
        shift(b_near_sides[1], "x", -1),
        shift(far[2], "x", 1),
    )
    more, down_own = lax.optimization_barrier((expert_slots(far, masks, weights), down_own))
    down_other = shift(down_own, "c", 1)
    slots = jnp.concatenate([slots, more, expert_slots(opposite, masks, weights, on_chip=True)], axis=0)
    active = ring(slots, "z")
    place = jnp.stack([x, y, z]).astype(jnp.int32)
    result = lower(place, active, down_own, down_other, chips)
    per_chip = result.shape[2]
    result = result.reshape(chips, 2 * per_chip, cols)
    returned = lax.all_to_all(result, ("x", "y"), 0, 0, tiled=True)

    rank = meta[:, :experts].astype(F32)
    weight = sum(meta[:, i * experts : (i + 1) * experts].astype(F32) for i in (1, 2, 3))
    by_core = lambda v: v.reshape(group, chips, 2)
    order = lambda v: jnp.where(c == 0, by_core(v), by_core(v)[:, :, ::-1])
    rank, weight = order(rank), order(weight)
    slot = jnp.arange(per_chip, dtype=jnp.int32)
    mine = (slot // CAP)[None, :] == (jnp.arange(group) // rows_n)[:, None]
    hit = mine[:, None, None, :] & (
        rank[..., None] == (slot % CAP).astype(F32)[None, None, None, :]
    )
    spread = jnp.where(hit, weight[..., None], 0.0).reshape(group, chips * 2 * per_chip)
    mixture = jnp.dot(
        spread,
        returned.reshape(chips * 2 * per_chip, cols).astype(F32),
        precision=lax.Precision.HIGHEST,
        preferred_element_type=F32,
    )
    block_tokens = lax.dynamic_slice(group_tokens, (jnp.int32(0), z * cols), (group, cols))
    stream_block = (block_tokens.astype(F32) + mixture).astype(BF)
    guard_args = (w_query, w_key, w_value, cache_keys[:, 0], cache_values[:, 0])
    group_stream = copies(stream_block, "z")
    stream, guard = attend(place, group_stream, *guard_args, lengths)
    return (stream, guard)


def solution(mesh):
    torus = Mesh(mesh.devices.reshape(4, 4, 2, mesh.devices.shape[1]), ("x", "y", "c", "z"))
    ep = ("x", "y", "c")
    every = (*ep, "z")
    return jax.shard_map(
        per_device,
        mesh=torus,
        in_specs=(
            P(every, None),
            P(every, None),
            P(every, None),
            P(ep, None, "z"),
            P(ep, None, "z"),
            P(ep, "z", None),
            P(None, "z"),
            P(None, "z"),
            P(None, "z"),
            P(ep, "z", None, None),
            P(ep, "z", None, None),
            P(ep),
        ),
        out_specs=(P(every, None), P(ep, "z")),
        check_vma=False,
    )
```
